256 devices in a mesh: outer: 8 (over y, core), inner: 32 (over z, x).
Axes of the slice: x: 4, y: 4, z: 8, core: 2. Of those that a mesh axis runs over, the one named last changes fastest.
Arguments:
- tokens: bfloat16 [98304, 4096], P(('outer', 'inner')), may hold values from -6 to 6
- out_grad: bfloat16 [98304, 1024], P(('outer', 'inner')), may hold values from -0.25 to 0.25
- master_weights: float32 [1024, 4096], P(('outer', 'inner')), may hold values from -0.0421 to 0.0421
- base_weights: bfloat16 [1024, 4096], replicated, may hold values from -0.030029297 to 0.030029297
- adam_m: float32 [1024, 4096], P(('outer', 'inner')), may hold values from -8 to 8
- adam_v: float32 [1024, 4096], P(('outer', 'inner')), may hold values from 0.1 to 10
- grad_exps: int32 [256, 8, 32], P(('outer', 'inner')), may hold values from -13 to -8
- diff_exps: int32 [1024, 32], P(('outer', 'inner')), may hold values from -20 to -15
- hadamard_signs: int32 [32, 128], replicated, may hold values 0 or 1
Outputs:
- projected: bfloat16 [98304, 1024], P(('outer', 'inner'))
- new_master: float32 [1024, 4096], P(('outer', 'inner'))
- new_first: float32 [1024, 4096], P(('outer', 'inner'))
- new_second: float32 [1024, 4096], P(('outer', 'inner'))
The draws below stay inside these ranges and needn't reach their ends.
All inputs are finite; a program needn't handle non-finite values.
Results may differ from the reference program's by a relative error of at most 0.005.
Values may be sent and summed in bfloat16 or wider, within the bound.
No kernel may reach another device: no remote copies, remote signals or barrier semaphores. Data moves between devices by JAX's collectives and lax.ppermute only.
A program may use at most 128 MiB of HBM per device.

```python
import math
import jax
import jax.numpy as jnp
from jax import lax

D = 4096
KV = 1024
HB = 128
ADAM_STEP = 10
TOK_DEV = 384
BLOCKS = 256
TOKENS = 98304


def shared_weights(key):
    base_key = jax.random.fold_in(key, 11)
    drift_key = jax.random.fold_in(key, 23)
    base_rows = jax.random.uniform(base_key, (KV, D), jnp.float32, -0.03, 0.03)
    drift_rows = jax.random.truncated_normal(drift_key, -4.0, 4.0, (KV, D), jnp.float32) * 0.003
    base_half = base_rows.astype(jnp.bfloat16)
    return (base_half, base_half.astype(jnp.float32) + drift_rows)


def draw_base_weights(key, part):
    return shared_weights(key)[0]


def draw_master_weights(key, part):
    return shared_weights(key)[1]


def with_ends(array, own_key, smallest, top_value):
    longest = array.shape.index(max(array.shape))
    spots = []
    for shift in (0, 1):
        where = [jax.random.randint(jax.random.fold_in(own_key, axis), (), 0, length) for axis, length in enumerate(array.shape)]
        where[longest] = (where[longest] + shift) % array.shape[longest]
        spots.append(tuple(where))
    return array.at[spots[0]].set(smallest).at[spots[1]].set(top_value)


def raised(result, key, source, target, shards_of, factor):
    def block_of(dim):
        return (jnp.arange(result.shape[dim]) // (result.shape[dim] // shards_of)).reshape((-1,) + (1,) * (result.ndim - 1 - dim))

    one_side = jax.random.permutation(key, shards_of)[block_of(target)]
    far = (block_of(target) + shards_of // 2) % shards_of
    return jnp.where((block_of(source) == one_side) | (block_of(source) == far), factor * result, result)


def levels(own_key, dims, cuts, smallest, high):
    level = 1.0
    for axis_at, blocks in cuts:
        draws = jax.random.uniform(jax.random.fold_in(jax.random.fold_in(own_key, 6), axis_at), (blocks,), jnp.float32, smallest / len(cuts), high / len(cuts))
        level = level * jnp.repeat(jnp.exp(draws), dims[axis_at] // blocks).reshape((-1,) + (1,) * (len(dims) - 1 - axis_at))
    return level


def gaussian(stream_key, shape, scale, reach, shards=(), held_as=jnp.bfloat16):
    factor_of = levels(stream_key, shape, shards, -0.22, 0.18) if shards else 1.0
    drawn = jax.random.normal(stream_key, shape, jnp.float32) * scale * factor_of
    return jnp.minimum(jnp.maximum(drawn, -reach), reach).astype(held_as)


def gaussian_with(own_key, dims, spread, limit, cuts, heavy, kind=jnp.bfloat16):
    array = spread * jax.random.normal(own_key, dims, jnp.float32)
    if cuts:
        array = array * levels(own_key, dims, cuts, -0.22, 0.18)
    return jnp.clip(raised(array, jax.random.fold_in(own_key, 3), *heavy), -limit, limit).astype(kind)


def setup_inputs(seed: int = 0) -> dict:
    seeds = jax.random.split(jax.random.key(seed), 10)
    tokens = gaussian(seeds[0], (TOKENS, D), 1.0, 6.0, ((0, 256),))
    out_grad = gaussian_with(seeds[1], (TOKENS, KV), (TOKENS // 9) ** -0.5, 0.25, ((0, 256),), (0, 1, 256, 6.0))
    master_weights = draw_master_weights(jax.random.fold_in(seeds[9], 71), 0)
    base_weights = draw_base_weights(jax.random.fold_in(seeds[9], 71), 0)
    adam_m = gaussian(seeds[4], (KV, D), 2.0, 8.0, ((0, 256),), jnp.float32)
    adam_v = jnp.clip(jnp.exp(math.log(10.0) - 4.6051702 * jax.random.uniform(seeds[5], (KV, D), jnp.float32) ** levels(seeds[5], (KV, D), ((0, 256),), -0.2, 0.2)), 0.1, 10.0)
    grad_exps = with_ends(jax.random.randint(seeds[6], (BLOCKS, KV // HB, D // HB), -13, -7), jax.random.fold_in(seeds[6], 1), -13, (-7) - 1).astype(jnp.int32)
    diff_exps = with_ends(jax.random.randint(seeds[7], (KV, D // HB), -20, -14), jax.random.fold_in(seeds[7], 1), -20, (-14) - 1).astype(jnp.int32)
    hadamard_signs = with_ends((jax.random.randint(seeds[8], (D // HB, HB), 0, 2) < 1).astype(jnp.int32), jax.random.fold_in(seeds[8], 1), 0, 1)
    return {"tokens": tokens, "out_grad": out_grad, "master_weights": master_weights, "base_weights": base_weights, "adam_m": adam_m, "adam_v": adam_v, "grad_exps": grad_exps, "diff_exps": diff_exps, "hadamard_signs": hadamard_signs}


clip_level = 448.0
beta_one = 0.9
beta_two = 0.95
learn_rate = 0.002
decay_rate = 0.1
adam_eps = 1e-08
highest = lax.Precision.HIGHEST

def hadamard(matrix_size):
    positions = jnp.arange(matrix_size, dtype=jnp.int32)
    common = positions[:, None] & positions[None, :]
    parity = jnp.zeros((matrix_size, matrix_size), jnp.int32)
    for bit_level in range(matrix_size.bit_length() - 1):
        parity = parity + (common >> bit_level & 1)
    return (1 - 2 * (parity % 2)).astype(jnp.float32)

def rotate_rows(row_block, sign_rows, matrix):
    row_count = row_block.shape[0]
    blocks = row_block.reshape(row_count, sign_rows.shape[0], sign_rows.shape[1]) * sign_rows
    turned = jnp.dot(blocks.reshape(-1, sign_rows.shape[1]), matrix, precision=highest)
    return turned.reshape(row_block.shape) / math.sqrt(sign_rows.shape[1])

def unrotate_rows(row_block, sign_rows, matrix):
    row_count = row_block.shape[0]
    turned = jnp.dot(row_block.reshape(-1, sign_rows.shape[1]), matrix, precision=highest) / math.sqrt(sign_rows.shape[1])
    return (turned.reshape(row_count, sign_rows.shape[0], sign_rows.shape[1]) * sign_rows).reshape(row_block.shape)

def clip_rows(row_block, bound_rows):
    row_count = row_block.shape[0]
    shaped = row_block.reshape(row_count, bound_rows.shape[1], -1)
    limits = bound_rows[:, :, None]
    return jnp.clip(shaped, -limits, limits).reshape(row_block.shape)

def adam_update(gradient, master, first, second):
    new_first = beta_one * first + (1.0 - beta_one) * gradient
    new_second = beta_two * second + (1.0 - beta_two) * gradient * gradient
    fix_one = 1.0 - beta_one ** ADAM_STEP
    fix_two = 1.0 - beta_two ** ADAM_STEP
    step_dir = new_first / fix_one / (jnp.sqrt(new_second / fix_two) + adam_eps)
    new_master = master - learn_rate * (step_dir + decay_rate * master)
    return (new_master, new_first, new_second)

def reference(tokens, out_grad, master_weights, base_weights, adam_m, adam_v, grad_exps, diff_exps, hadamard_signs):
    sign_rows = (2 * hadamard_signs - 1).astype(jnp.float32)
    matrix = hadamard(HB)

    def add_block(total, block_id):
        rows_x = lax.dynamic_slice_in_dim(tokens, block_id * TOK_DEV, TOK_DEV, 0)
        rows_g = lax.dynamic_slice_in_dim(out_grad, block_id * TOK_DEV, TOK_DEV, 0)
        term_rows = lax.dot_general(rows_g, rows_x, (((0,), (0,)), ((), ())), preferred_element_type=jnp.float32)
        turned = rotate_rows(term_rows, sign_rows, matrix)
        exps_here = lax.dynamic_index_in_dim(grad_exps, block_id, 0, keepdims=False)
        bound_rows = jnp.repeat(clip_level * jnp.exp2(exps_here.astype(jnp.float32)), HB, axis=0)
        coded_rows = lax.optimization_barrier(clip_rows(turned, bound_rows).astype(jnp.bfloat16))
        return (total + coded_rows.astype(jnp.float32), None)
    summed, unused = lax.scan(add_block, jnp.zeros((KV, D), jnp.float32), jnp.arange(BLOCKS, dtype=jnp.int32))
    gradient = unrotate_rows(summed, sign_rows, matrix)
    new_master, new_first, new_second = adam_update(gradient, master_weights, adam_m, adam_v)
    base_full = base_weights.astype(jnp.float32)
    diff_bound = clip_level * jnp.exp2(diff_exps.astype(jnp.float32))
    diff_coded = lax.optimization_barrier(clip_rows(new_master - base_full, diff_bound).astype(jnp.bfloat16))
    effective = (base_full + diff_coded.astype(jnp.float32)).astype(jnp.bfloat16)
    projected = lax.dot_general(tokens, effective, (((1,), (1,)), ((), ())), preferred_element_type=jnp.float32)
    return (projected.astype(jnp.bfloat16), new_master, new_first, new_second)
```

```python
import math

import jax
import jax.numpy as jnp
from jax import lax
from jax.experimental import pallas as pl
from jax.experimental.pallas import tpu as pltpu
from jax.sharding import Mesh
from jax.sharding import PartitionSpec as P

ADAM_STEP = 10
OUTER_INNER = ("outer", "inner_0", "inner_1")

clip_level = 448.0
beta_one = 0.9
beta_two = 0.95
learn_rate = 0.002
decay_rate = 0.1
adam_eps = 1e-08
highest = lax.Precision.HIGHEST


def hadamard(matrix_size):
    positions = jnp.arange(matrix_size, dtype=jnp.int32)
    common = positions[:, None] & positions[None, :]
    parity = jnp.zeros((matrix_size, matrix_size), jnp.int32)
    for bit_level in range(matrix_size.bit_length() - 1):
        parity = parity + (common >> bit_level & 1)
    return (1 - 2 * (parity % 2)).astype(jnp.float32)


def unrotate_rows(row_block, sign_rows, matrix):
    row_count = row_block.shape[0]
    turned = jnp.dot(
        row_block.reshape(-1, sign_rows.shape[1]), matrix, precision=highest
    ) / math.sqrt(sign_rows.shape[1])
    return (turned.reshape(row_count, sign_rows.shape[0], sign_rows.shape[1]) * sign_rows).reshape(
        row_block.shape
    )


def clip_rows(row_block, bound_rows):
    row_count = row_block.shape[0]
    shaped = row_block.reshape(row_count, bound_rows.shape[1], -1)
    limits = bound_rows[:, :, None]
    return jnp.clip(shaped, -limits, limits).reshape(row_block.shape)


def adam_update(gradient, master, first, second):
    new_first = beta_one * first + (1.0 - beta_one) * gradient
    new_second = beta_two * second + (1.0 - beta_two) * gradient * gradient
    fix_one = 1.0 - beta_one**ADAM_STEP
    fix_two = 1.0 - beta_two**ADAM_STEP
    step_dir = new_first / fix_one / (jnp.sqrt(new_second / fix_two) + adam_eps)
    new_master = master - learn_rate * (step_dir + decay_rate * master)
    return (new_master, new_first, new_second)


def coded_kernel(block_len, row_tile, tok_ref, grad_ref, sign_ref, bound_ref, mat_ref, out_ref, turned_ref, grad_t_ref):
    token_rows = tok_ref.shape[0]
    width = tok_ref.shape[1]

    @pl.when(pl.program_id(0) == 0)
    def _():
        grad_t = grad_ref[...].T
        grad_t_ref[:, :token_rows] = grad_t
        grad_t_ref[:, token_rows:] = grad_t

    scale = 1.0 / math.sqrt(block_len)
    for start in range(0, width, block_len):
        cols = slice(start, start + block_len)
        signed = tok_ref[:, cols] * sign_ref[:, cols]
        turned = jnp.dot(signed, mat_ref[...], preferred_element_type=jnp.float32) * scale
        upper = turned.astype(jnp.bfloat16)
        turned_ref[:token_rows, cols] = upper
        turned_ref[token_rows:, cols] = (turned - upper.astype(jnp.float32)).astype(jnp.bfloat16)
    terms = jnp.dot(grad_t_ref[...], turned_ref[...], preferred_element_type=jnp.float32)
    for tile in range(out_ref.shape[0] // row_tile):
        rows = slice(tile * row_tile, (tile + 1) * row_tile)
        limit = bound_ref[tile : tile + 1, :]
        out_ref[rows, :] = jnp.clip(terms[rows, :], -limit, limit).astype(jnp.bfloat16)


def coded_gradient(tokens, out_grad, signs, bounds, matrix):
    token_rows, model_width = tokens.shape
    feature_rows = out_grad.shape[1]
    block_len = matrix.shape[0]
    width = 512
    row_tile = feature_rows // bounds.shape[0]
    body = lambda *refs: coded_kernel(block_len, row_tile, *refs)
    return pl.pallas_call(
        body,
        grid=(model_width // width,),
        in_specs=[
            pl.BlockSpec((token_rows, width), lambda n: (0, n)),
            pl.BlockSpec((token_rows, feature_rows), lambda n: (0, 0)),
            pl.BlockSpec((1, width), lambda n: (0, n)),
            pl.BlockSpec((bounds.shape[0], width), lambda n: (0, n)),
            pl.BlockSpec((block_len, block_len), lambda n: (0, 0)),
        ],
        out_specs=pl.BlockSpec((feature_rows, width), lambda n: (0, n)),
        out_shape=jax.ShapeDtypeStruct((feature_rows, model_width), jnp.bfloat16),
        scratch_shapes=[
            pltpu.VMEM((2 * token_rows, width), jnp.bfloat16),
            pltpu.VMEM((feature_rows, 2 * token_rows), jnp.bfloat16),
        ],
        compiler_params=pltpu.CompilerParams(vmem_limit_bytes=48 << 20),
    )(tokens, out_grad, signs, bounds, matrix)


def shards(
    tokens,
    out_grad,
    master_weights,
    base_weights,
    adam_m,
    adam_v,
    grad_exps,
    diff_exps,
    hadamard_signs,
):
    rows_dev = master_weights.shape[0]
    sign_rows = (2 * hadamard_signs - 1).astype(jnp.float32)
    block_len = sign_rows.shape[1]
    matrix = hadamard(block_len)
    bounds = jnp.repeat(clip_level * jnp.exp2(grad_exps[0].astype(jnp.float32)), block_len, axis=1)
    coded = coded_gradient(
        tokens,
        out_grad,
        sign_rows.reshape(1, -1).astype(jnp.bfloat16),
        bounds,
        matrix.astype(jnp.bfloat16),
    )
    for axis in OUTER_INNER:
        coded = lax.psum_scatter(coded, axis, scatter_dimension=0, tiled=True)
    gradient = unrotate_rows(coded.astype(jnp.float32), sign_rows, matrix)
    new_master, new_first, new_second = adam_update(gradient, master_weights, adam_m, adam_v)
    owner = lax.axis_index(OUTER_INNER)
    base_own = lax.dynamic_slice_in_dim(base_weights, owner * rows_dev, rows_dev, 0).astype(
        jnp.float32
    )
    diff_bound = clip_level * jnp.exp2(diff_exps.astype(jnp.float32))
    diff_coded = clip_rows(new_master - base_own, diff_bound).astype(jnp.bfloat16)
    effective = (base_own + diff_coded.astype(jnp.float32)).astype(jnp.bfloat16)
    for axis in reversed(OUTER_INNER):
        effective = lax.all_gather(effective, axis, axis=0, tiled=True)
    projected = lax.dot_general(
        tokens, effective, (((1,), (1,)), ((), ())), preferred_element_type=jnp.float32
    ).astype(jnp.bfloat16)
    return (projected, new_master, new_first, new_second)


def solution(mesh):
    split = Mesh(mesh.devices.reshape(mesh.shape["outer"], 8, 4), OUTER_INNER)
    rows = P(OUTER_INNER, None)
    return jax.shard_map(
        shards,
        mesh=split,
        in_specs=(rows, rows, rows, P(), rows, rows, P(OUTER_INNER, None, None), rows, P()),
        out_specs=(rows, rows, rows, rows),
        check_vma=False,
    )
```

```python
import math

import jax
import jax.numpy as jnp
from jax import lax
from jax.experimental import pallas as pl
from jax.experimental.pallas import tpu as pltpu
from jax.sharding import Mesh
from jax.sharding import PartitionSpec as P

ADAM_STEP = 10
AXES = ("y", "c", "z", "x")
FACE = ("y", "c", "x")

clip_level = 448.0
beta_one = 0.9
beta_two = 0.95
learn_rate = 0.002
decay_rate = 0.1
adam_eps = 1e-08
highest = lax.Precision.HIGHEST


def hadamard(matrix_size):
    positions = jnp.arange(matrix_size, dtype=jnp.int32)
    common = positions[:, None] & positions[None, :]
    parity = jnp.zeros((matrix_size, matrix_size), jnp.int32)
    for bit_level in range(matrix_size.bit_length() - 1):
        parity = parity + (common >> bit_level & 1)
    return (1 - 2 * (parity % 2)).astype(jnp.float32)


def unrotate_rows(row_block, sign_rows, matrix):
    row_count = row_block.shape[0]
    turned = jnp.dot(
        row_block.reshape(-1, sign_rows.shape[1]), matrix, precision=highest
    ) / math.sqrt(sign_rows.shape[1])
    return (turned.reshape(row_count, sign_rows.shape[0], sign_rows.shape[1]) * sign_rows).reshape(
        row_block.shape
    )


def clip_rows(row_block, bound_rows):
    row_count = row_block.shape[0]
    shaped = row_block.reshape(row_count, bound_rows.shape[1], -1)
    limits = bound_rows[:, :, None]
    return jnp.clip(shaped, -limits, limits).reshape(row_block.shape)


def adam_update(gradient, master, first, second):
    new_first = beta_one * first + (1.0 - beta_one) * gradient
    new_second = beta_two * second + (1.0 - beta_two) * gradient * gradient
    fix_one = 1.0 - beta_one**ADAM_STEP
    fix_two = 1.0 - beta_two**ADAM_STEP
    step_dir = new_first / fix_one / (jnp.sqrt(new_second / fix_two) + adam_eps)
    new_master = master - learn_rate * (step_dir + decay_rate * master)
    return (new_master, new_first, new_second)


def row_order(count_z, count_x, rows_dev):
    size = count_z * count_x * rows_dev
    spots = jnp.arange(size, dtype=jnp.int32)
    at_x, at_z, at_j = spots // (count_z * rows_dev), spots // rows_dev % count_z, spots % rows_dev
    natural = (at_z * count_x + at_x) * rows_dev + at_j
    return (natural[:, None] == spots[None, :]).astype(jnp.bfloat16)


def coded_kernel(groups, added, core_ref, tok_ref, *refs):
    grad_refs = refs[:groups]
    sign_ref, bound_ref, mat_ref, order_ref = refs[groups : groups + 4]
    if added:
        own_ref, out_ref, turned_ref, grad_t_ref = refs[groups + 4 :]
    else:
        out_ref, turned_ref, grad_t_ref = refs[groups + 4 :]
    token_rows, width = tok_ref.shape
    block_len = mat_ref.shape[0]
    tile = order_ref.shape[0]
    core = core_ref[0]

    @pl.when(pl.program_id(0) == 0)
    def _():
        for group in range(groups):
            grad_t = lax.dot_general(
                order_ref[...],
                grad_refs[group][...],
                (((1,), (1,)), ((), ())),
                preferred_element_type=jnp.float32,
            ).astype(jnp.bfloat16)
            rows = slice(group * tile, (group + 1) * tile)
            grad_t_ref[rows, :token_rows] = grad_t
            grad_t_ref[rows, token_rows:] = grad_t

    scale = 1.0 / math.sqrt(block_len)
    for start in range(0, width, block_len):
        cols = slice(start, start + block_len)
        signed = tok_ref[:, cols] * sign_ref[:, cols]
        turned = jnp.dot(signed, mat_ref[...], preferred_element_type=jnp.float32) * scale
        upper = turned.astype(jnp.bfloat16)
        turned_ref[:token_rows, cols] = upper
        turned_ref[token_rows:, cols] = (turned - upper.astype(jnp.float32)).astype(jnp.bfloat16)
    terms = jnp.dot(grad_t_ref[...], turned_ref[...], preferred_element_type=jnp.float32)
    for group in range(groups):
        rows = slice(group * tile, (group + 1) * tile)
        limit = bound_ref[pl.ds(2 * group + core, 1), :]
        coded = jnp.clip(terms[rows, :], -limit, limit).astype(jnp.bfloat16)
        if not added:
            out_ref[rows, :] = coded
            continue
        total = (coded.astype(jnp.float32) + own_ref[rows, :].astype(jnp.float32)).astype(
            jnp.bfloat16
        )
        part = out_ref.shape[2]
        for spot in range(tile // part):
            first = jnp.where(core == 0, spot, group)
            second = jnp.where(core == 0, group, spot)
            out_ref[first, second] = total[spot * part : (spot + 1) * part]


def coded_gradient(core, tokens, out_grad, signs, bounds, matrix, order, own=None, count=1):
    token_rows, model_width = tokens.shape
    feature_rows = out_grad.shape[1]
    tile = order.shape[0]
    groups = feature_rows // tile // 2
    width = 512
    added = own is not None
    if added:
        part = tile // count
        out_shape = (count, groups, part, model_width)
        out_spec = pl.BlockSpec((count, groups, part, width), lambda n, core: (0, 0, 0, n))
    else:
        out_shape = (groups * tile, model_width)
        out_spec = pl.BlockSpec((groups * tile, width), lambda n, core: (0, n))
    whole = lambda n, core: (0, 0)
    column = lambda n, core: (0, n)
    grad_spec = lambda group: pl.BlockSpec(
        (token_rows, tile), lambda n, core: (0, 2 * group + core[0])
    )
    in_specs = [
        pl.BlockSpec((token_rows, width), column),
        *[grad_spec(group) for group in range(groups)],
        pl.BlockSpec((1, width), column),
        pl.BlockSpec((bounds.shape[0], width), column),
        pl.BlockSpec(matrix.shape, whole),
        pl.BlockSpec(order.shape, whole),
    ]
    operands = [tokens, *[out_grad] * groups, signs, bounds, matrix, order]
    if added:
        in_specs.append(pl.BlockSpec((groups * tile, width), column))
        operands.append(own)
    body = lambda *refs: coded_kernel(groups, added, *refs)
    return pl.pallas_call(
        body,
        grid_spec=pltpu.PrefetchScalarGridSpec(
            num_scalar_prefetch=1,
            grid=(model_width // width,),
            in_specs=in_specs,
            out_specs=out_spec,
            scratch_shapes=[
                pltpu.VMEM((2 * token_rows, width), jnp.bfloat16),
                pltpu.VMEM((groups * tile, 2 * token_rows), jnp.bfloat16),
            ],
        ),
        out_shape=jax.ShapeDtypeStruct(out_shape, jnp.bfloat16),
        compiler_params=pltpu.CompilerParams(vmem_limit_bytes=24 << 20),
    )(core, *operands)


def project_kernel(pair, core_ref, tok_ref, weight_ref, order_ref, out_ref):
    tile = order_ref.shape[0]
    core = core_ref[0]
    rows = []
    for at in range(pair):
        group = pl.program_id(0) * pair + at
        for spot in range(tile // weight_ref.shape[2]):
            first = jnp.where(core == 0, spot, group)
            second = jnp.where(core == 0, group, spot)
            rows.append(weight_ref[first, second])
    total = lax.dot_general(
        tok_ref[...],
        jnp.concatenate(rows, axis=0),
        (((1,), (1,)), ((), ())),
        preferred_element_type=jnp.float32,
    )
    rounded = total.astype(jnp.bfloat16)
    for at in range(pair):
        cols = slice(at * tile, (at + 1) * tile)
        out_ref[:, cols] = jnp.dot(
            rounded[:, cols], order_ref[...], preferred_element_type=jnp.float32
        ).astype(jnp.bfloat16)


def project(core, tokens, weights, order, groups):
    token_rows = tokens.shape[0]
    tile = order.shape[0]
    pair = 2
    body = lambda *refs: project_kernel(pair, *refs)
    return pl.pallas_call(
        body,
        grid_spec=pltpu.PrefetchScalarGridSpec(
            num_scalar_prefetch=1,
            grid=(groups // pair,),
            in_specs=[
                pl.BlockSpec(tokens.shape, lambda n, core: (0, 0)),
                pl.BlockSpec(weights.shape, lambda n, core: (0, 0, 0, 0)),
                pl.BlockSpec(order.shape, lambda n, core: (0, 0)),
            ],
            out_specs=pl.BlockSpec((token_rows, pair * tile), lambda n, core: (0, n)),
        ),
        out_shape=jax.ShapeDtypeStruct((token_rows, groups * tile), jnp.bfloat16),
        compiler_params=pltpu.CompilerParams(vmem_limit_bytes=32 << 20),
    )(core, tokens, weights, order)


def interleave_kernel(core_ref, own_ref, peer_ref, out_ref):
    tile = own_ref.shape[1]
    first = core_ref[0] == 0
    out_ref[:, :tile] = jnp.where(first, own_ref[...], peer_ref[...])
    out_ref[:, tile:] = jnp.where(first, peer_ref[...], own_ref[...])


def interleaved(core, own_part, peer_part, tile):
    rows, width = own_part.shape
    spec = pl.BlockSpec((rows, tile), lambda n, core: (0, n))
    return pl.pallas_call(
        interleave_kernel,
        grid_spec=pltpu.PrefetchScalarGridSpec(
            num_scalar_prefetch=1,
            grid=(width // tile,),
            in_specs=[spec, spec],
            out_specs=pl.BlockSpec((rows, 2 * tile), lambda n, core: (0, n)),
        ),
        out_shape=jax.ShapeDtypeStruct((rows, 2 * width), jnp.bfloat16),
    )(core, own_part, peer_part)


def swapped(value):
    return lax.ppermute(value, "c", [(0, 1), (1, 0)])


def face_groups(first):
    at = lambda y, c, x: (y * 2 + c) * 4 + x
    groups = []
    for core in (0, 1):
        for line in range(4):
            if (core == 0) == first:
                groups.append([at(line, core, spot) for spot in range(4)])
            else:
                groups.append([at(spot, core, line) for spot in range(4)])
    return groups


def exchanged(value, step):
    if step == "z":
        return lax.all_to_all(value, "z", 0, 0, tiled=True)
    return lax.all_to_all(
        value, FACE, 0, 0, tiled=True, axis_index_groups=face_groups(step == "first")
    )


def reduced(value, step):
    return jnp.sum(exchanged(value, step).astype(jnp.float32), axis=0)


def gathered(value, count, step):
    return exchanged(jnp.broadcast_to(value[None], (count, *value.shape)), step)


def shards(
    tokens,
    out_grad,
    master_weights,
    base_weights,
    adam_m,
    adam_v,
    grad_exps,
    diff_exps,
    hadamard_signs,
):
    count_y, count_z, count_x = (lax.axis_size(axis) for axis in ("y", "z", "x"))
    rows_dev, model_width = master_weights.shape
    sign_rows = (2 * hadamard_signs - 1).astype(jnp.float32)
    block_len = sign_rows.shape[1]
    matrix = hadamard(block_len)
    order = row_order(count_z, count_x, rows_dev)
    core = lax.axis_index("c")
    core_at = core.reshape(1).astype(jnp.int32)
    limits = clip_level * jnp.exp2(grad_exps[0].astype(jnp.float32))
    peer_tokens, peer_grad, peer_limits = swapped(tokens), swapped(out_grad), swapped(limits)
    signs = sign_rows.reshape(1, -1).astype(jnp.bfloat16)
    half_matrix = matrix.astype(jnp.bfloat16)
    own = coded_gradient(
        core_at, tokens, out_grad, signs, jnp.repeat(limits, block_len, axis=1), half_matrix, order
    )
    pair_sum = coded_gradient(
        core_at,
        peer_tokens,
        peer_grad,
        signs,
        jnp.repeat(peer_limits, block_len, axis=1),
        half_matrix,
        order,
        own=own,
        count=count_x,
    )
    line_sum = reduced(pair_sum, "first").astype(jnp.bfloat16)
    face_sum = reduced(line_sum, "second").astype(jnp.bfloat16)
    summed = reduced(face_sum.reshape(count_z, rows_dev, model_width), "z")
    gradient = unrotate_rows(summed, sign_rows, matrix)
    new_master, new_first, new_second = adam_update(gradient, master_weights, adam_m, adam_v)
    owner = lax.axis_index(AXES)
    base_own = lax.dynamic_slice_in_dim(base_weights, owner * rows_dev, rows_dev, 0).astype(
        jnp.float32
    )
    diff_bound = clip_level * jnp.exp2(diff_exps.astype(jnp.float32))
    diff_coded = clip_rows(new_master - base_own, diff_bound).astype(jnp.bfloat16)
    effective = (base_own + diff_coded.astype(jnp.float32)).astype(jnp.bfloat16)
    stacked = gathered(effective, count_z, "z").reshape(count_z * rows_dev, model_width)
    weights = gathered(gathered(stacked, count_y, "second"), count_x, "first")
    peer_part = swapped(project(core_at, peer_tokens, weights, order, count_y))
    own_part = project(core_at, tokens, weights, order, count_y)
    projected = interleaved(core_at, own_part, peer_part, order.shape[0])
    return (projected, new_master, new_first, new_second)


def solution(mesh):
    split = Mesh(mesh.devices.reshape(4, 2, 8, 4), AXES)
    rows = P(AXES, None)
    return jax.shard_map(
        shards,
        mesh=split,
        in_specs=(rows, rows, rows, P(), rows, rows, P(AXES, None, None), rows, P()),
        out_specs=(rows, rows, rows, rows),
        check_vma=False,
    )
```

```python
import math

import jax
import jax.numpy as jnp
import numpy as np
from jax import lax
from jax.experimental import pallas as pl
from jax.experimental.pallas import tpu as pltpu
from jax.sharding import Mesh
from jax.sharding import PartitionSpec as P

ADAM_STEP = 10
AXES = ("y", "c", "z", "x")
FACE = ("y", "c", "x")

clip_level = 448.0
beta_one = 0.9
beta_two = 0.95
learn_rate = 0.002
decay_rate = 0.1
adam_eps = 1e-08
highest = lax.Precision.HIGHEST


def hadamard(matrix_size):
    positions = np.arange(matrix_size)
    common = positions[:, None] & positions[None, :]
    parity = np.zeros((matrix_size, matrix_size), np.int32)
    for bit_level in range(matrix_size.bit_length() - 1):
        parity = parity + (common >> bit_level & 1)
    return (1 - 2 * (parity % 2)).astype(np.float32)


def unrotate_rows(row_block, sign_rows, matrix):
    row_count = row_block.shape[0]
    turned = jnp.dot(
        row_block.reshape(-1, sign_rows.shape[1]), matrix, precision=highest
    ) / math.sqrt(sign_rows.shape[1])
    return (turned.reshape(row_count, sign_rows.shape[0], sign_rows.shape[1]) * sign_rows).reshape(
        row_block.shape
    )


def clip_rows(row_block, bound_rows):
    row_count = row_block.shape[0]
    shaped = row_block.reshape(row_count, bound_rows.shape[1], -1)
    limits = bound_rows[:, :, None]
    return jnp.clip(shaped, -limits, limits).reshape(row_block.shape)


def adam_update(gradient, master, first, second):
    new_first = beta_one * first + (1.0 - beta_one) * gradient
    new_second = beta_two * second + (1.0 - beta_two) * gradient * gradient
    fix_one = 1.0 - beta_one**ADAM_STEP
    fix_two = 1.0 - beta_two**ADAM_STEP
    step_dir = new_first / fix_one / (jnp.sqrt(new_second / fix_two) + adam_eps)
    new_master = master - learn_rate * (step_dir + decay_rate * master)
    return (new_master, new_first, new_second)


def row_order(count_z, count_x, rows_dev):
    size = count_z * count_x * rows_dev
    spots = np.arange(size)
    at_x, at_z, at_j = spots // (count_z * rows_dev), spots // rows_dev % count_z, spots % rows_dev
    natural = (at_z * count_x + at_x) * rows_dev + at_j
    return (natural[:, None] == spots[None, :]).astype(np.float32)


def coded_kernel(groups, added, core_ref, tok_ref, *refs):
    grad_refs = refs[:groups]
    sign_ref, exps_ref, mat_ref, order_ref = refs[groups : groups + 4]
    if added:
        own_ref, out_ref, turned_ref, grad_t_ref, limit_ref = refs[groups + 4 :]
    else:
        out_ref, turned_ref, grad_t_ref, limit_ref = refs[groups + 4 :]
    token_rows, width = tok_ref.shape
    block_len = mat_ref.shape[0]
    tile = order_ref.shape[0]
    core = core_ref[0]
    first_block = pl.program_id(0) * (width // block_len)

    @pl.when(pl.program_id(0) == 0)
    def _():
        for group in range(groups):
            grad_t = lax.dot_general(
                order_ref[...],
                grad_refs[group][...],
                (((1,), (1,)), ((), ())),
                preferred_element_type=jnp.float32,
            ).astype(jnp.bfloat16)
            rows = slice(group * tile, (group + 1) * tile)
            grad_t_ref[rows, :token_rows] = grad_t
            grad_t_ref[rows, token_rows:] = grad_t

    levels = (clip_level * jnp.exp2(exps_ref[...].astype(jnp.float32))).astype(jnp.bfloat16)
    spread_shape = (exps_ref.shape[1], width)
    block_at = lax.broadcasted_iota(jnp.int32, spread_shape, 0) - first_block
    lane_at = lax.broadcasted_iota(jnp.int32, spread_shape, 1)
    start_at = block_at * block_len
    inside = (lane_at >= start_at) & (lane_at < start_at + block_len)
    spread = jnp.where(inside, 1.0, 0.0).astype(jnp.bfloat16)
    limit_ref[...] = jnp.dot(levels, spread, preferred_element_type=jnp.float32)

    scale = 1.0 / math.sqrt(block_len)
    for block in range(width // block_len):
        cols = slice(block * block_len, (block + 1) * block_len)
        signs = 2 * sign_ref[pl.ds(first_block + block, 1), :] - 1
        signed = tok_ref[:, cols] * signs.astype(jnp.float32).astype(jnp.bfloat16)
        turned = jnp.dot(signed, mat_ref[...], preferred_element_type=jnp.float32) * scale
        upper = turned.astype(jnp.bfloat16)
        turned_ref[:token_rows, cols] = upper
        turned_ref[token_rows:, cols] = (turned - upper.astype(jnp.float32)).astype(jnp.bfloat16)
    terms = jnp.dot(grad_t_ref[...], turned_ref[...], preferred_element_type=jnp.float32)
    for group in range(groups):
        rows = slice(group * tile, (group + 1) * tile)
        limit = limit_ref[pl.ds(2 * group + core, 1), :]
        coded = jnp.clip(terms[rows, :], -limit, limit).astype(jnp.bfloat16)
        if not added:
            out_ref[rows, :] = coded
            continue
        total = (coded.astype(jnp.float32) + own_ref[rows, :].astype(jnp.float32)).astype(
            jnp.bfloat16
        )
        part = out_ref.shape[2]
        for spot in range(tile // part):
            first = jnp.where(core == 0, spot, group)
            second = jnp.where(core == 0, group, spot)
            out_ref[first, second] = total[spot * part : (spot + 1) * part]


def coded_gradient(core, tokens, out_grad, signs, exps, matrix, order, own=None, count=1):
    token_rows, model_width = tokens.shape
    feature_rows = out_grad.shape[1]
    tile = order.shape[0]
    groups = feature_rows // tile // 2
    width = 1024
    added = own is not None
    if added:
        part = tile // count
        out_shape = (count, groups, part, model_width)
        out_spec = pl.BlockSpec((count, groups, part, width), lambda n, core: (0, 0, 0, n))
    else:
        out_shape = (groups * tile, model_width)
        out_spec = pl.BlockSpec((groups * tile, width), lambda n, core: (0, n))
    whole = lambda n, core: (0, 0)
    column = lambda n, core: (0, n)
    grad_spec = lambda group: pl.BlockSpec(
        (token_rows, tile), lambda n, core: (0, 2 * group + core[0])
    )
    in_specs = [
        pl.BlockSpec((token_rows, width), column),
        *[grad_spec(group) for group in range(groups)],
        pl.BlockSpec(signs.shape, whole),
        pl.BlockSpec(exps.shape, whole),
        pl.BlockSpec(matrix.shape, whole),
        pl.BlockSpec(order.shape, whole),
    ]
    operands = [tokens, *[out_grad] * groups, signs, exps, matrix, order]
    if added:
        in_specs.append(pl.BlockSpec((groups * tile, width), column))
        operands.append(own)
    body = lambda *refs: coded_kernel(groups, added, *refs)
    return pl.pallas_call(
        body,
        grid_spec=pltpu.PrefetchScalarGridSpec(
            num_scalar_prefetch=1,
            grid=(model_width // width,),
            in_specs=in_specs,
            out_specs=out_spec,
            scratch_shapes=[
                pltpu.VMEM((2 * token_rows, width), jnp.bfloat16),
                pltpu.VMEM((groups * tile, 2 * token_rows), jnp.bfloat16),
                pltpu.VMEM((exps.shape[0], width), jnp.float32),
            ],
        ),
        out_shape=jax.ShapeDtypeStruct(out_shape, jnp.bfloat16),
        compiler_params=pltpu.CompilerParams(vmem_limit_bytes=(44 if added else 60) << 20),
    )(core, *operands)


def sum_kernel(parts_ref, out_ref):
    total = parts_ref[0].astype(jnp.float32)
    for at in range(1, parts_ref.shape[0]):
        total = total + parts_ref[at].astype(jnp.float32)
    out_ref[...] = total.astype(jnp.bfloat16)


def summed_parts(parts):
    count, groups, part, model_width = parts.shape
    width = 1024
    return pl.pallas_call(
        sum_kernel,
        grid=(model_width // width,),
        in_specs=[pl.BlockSpec((count, groups, part, width), lambda n: (0, 0, 0, n))],
        out_specs=pl.BlockSpec((groups, part, width), lambda n: (0, 0, n)),
        out_shape=jax.ShapeDtypeStruct((groups, part, model_width), jnp.bfloat16),
        compiler_params=pltpu.CompilerParams(vmem_limit_bytes=16 << 20),
    )(parts)


def project_kernel(pair, core_ref, tok_ref, weight_ref, order_ref, out_ref):
    tile = order_ref.shape[0]
    core = core_ref[0]
    rows = []
    for at in range(pair):
        group = pl.program_id(0) * pair + at
        for spot in range(tile // weight_ref.shape[2]):
            first = jnp.where(core == 0, spot, group)
            second = jnp.where(core == 0, group, spot)
            rows.append(weight_ref[first, second])
    total = lax.dot_general(
        tok_ref[...],
        jnp.concatenate(rows, axis=0),
        (((1,), (1,)), ((), ())),
        preferred_element_type=jnp.float32,
    )
    rounded = total.astype(jnp.bfloat16)
    for at in range(pair):
        cols = slice(at * tile, (at + 1) * tile)
        out_ref[:, cols] = jnp.dot(
            rounded[:, cols], order_ref[...], preferred_element_type=jnp.float32
        ).astype(jnp.bfloat16)


def project(core, tokens, weights, order, groups):
    token_rows = tokens.shape[0]
    tile = order.shape[0]
    pair = 2
    body = lambda *refs: project_kernel(pair, *refs)
    return pl.pallas_call(
        body,
        grid_spec=pltpu.PrefetchScalarGridSpec(
            num_scalar_prefetch=1,
            grid=(groups // pair,),
            in_specs=[
                pl.BlockSpec(tokens.shape, lambda n, core: (0, 0)),
                pl.BlockSpec(weights.shape, lambda n, core: (0, 0, 0, 0)),
                pl.BlockSpec(order.shape, lambda n, core: (0, 0)),
            ],
            out_specs=pl.BlockSpec((token_rows, pair * tile), lambda n, core: (0, n)),
        ),
        out_shape=jax.ShapeDtypeStruct((token_rows, groups * tile), jnp.bfloat16),
        compiler_params=pltpu.CompilerParams(vmem_limit_bytes=32 << 20),
    )(core, tokens, weights, order)


def interleave_kernel(core_ref, own_ref, peer_ref, out_ref):
    tile = 128
    first = core_ref[0] == 0
    for group in range(own_ref.shape[1] // tile):
        cols = slice(group * tile, (group + 1) * tile)
        own, peer = own_ref[:, cols], peer_ref[:, cols]
        start = 2 * group * tile
        out_ref[:, start : start + tile] = jnp.where(first, own, peer)
        out_ref[:, start + tile : start + 2 * tile] = jnp.where(first, peer, own)


def interleaved(core, own_part, peer_part):
    rows, width = own_part.shape
    whole = pl.BlockSpec(memory_space=pltpu.VMEM)
    return pl.pallas_call(
        interleave_kernel,
        in_specs=[pl.BlockSpec(memory_space=pltpu.SMEM), whole, whole],
        out_specs=whole,
        out_shape=jax.ShapeDtypeStruct((rows, 2 * width), jnp.bfloat16),
        compiler_params=pltpu.CompilerParams(vmem_limit_bytes=8 << 20),
    )(core, own_part, peer_part)


def swapped(value):
    return lax.ppermute(value, "c", [(0, 1), (1, 0)])


def face_groups(first):
    at = lambda y, c, x: (y * 2 + c) * 4 + x
    groups = []
    for core in (0, 1):
        for line in range(4):
            if (core == 0) == first:
                groups.append([at(line, core, spot) for spot in range(4)])
            else:
                groups.append([at(spot, core, line) for spot in range(4)])
    return groups


def exchanged(value, step):
    if step == "z":
        return lax.all_to_all(value, "z", 0, 0, tiled=True)
    return lax.all_to_all(
        value, FACE, 0, 0, tiled=True, axis_index_groups=face_groups(step == "first")
    )


def reduced(value, step):
    return jnp.sum(exchanged(value, step).astype(jnp.float32), axis=0)


def gathered(value, count, step):
    return exchanged(jnp.broadcast_to(value[None], (count, *value.shape)), step)


def shards(
    tokens,
    out_grad,
    master_weights,
    base_weights,
    adam_m,
    adam_v,
    grad_exps,
    diff_exps,
    hadamard_signs,
):
    count_y, count_z, count_x = (lax.axis_size(axis) for axis in ("y", "z", "x"))
    rows_dev, model_width = master_weights.shape
    sign_rows = (2 * hadamard_signs - 1).astype(jnp.float32)
    block_len = sign_rows.shape[1]
    matrix = jnp.asarray(hadamard(block_len))
    order = jnp.asarray(row_order(count_z, count_x, rows_dev))
    core = lax.axis_index("c")
    core_at = core.reshape(1).astype(jnp.int32)
    exps = grad_exps[0]
    peer_tokens, peer_grad, peer_exps = swapped(tokens), swapped(out_grad), swapped(exps)
    half_matrix, order = matrix.astype(jnp.bfloat16), order.astype(jnp.bfloat16)
    own = coded_gradient(core_at, tokens, out_grad, hadamard_signs, exps, half_matrix, order)
    pair_sum = coded_gradient(
        core_at,
        peer_tokens,
        peer_grad,
        hadamard_signs,
        peer_exps,
        half_matrix,
        order,
        own=own,
        count=count_x,
    )
    line_sum = summed_parts(exchanged(pair_sum, "first"))
    face_sum = reduced(line_sum, "second").astype(jnp.bfloat16)
    summed = reduced(face_sum.reshape(count_z, rows_dev, model_width), "z")
    gradient = unrotate_rows(summed, sign_rows, matrix)
    new_master, new_first, new_second = adam_update(gradient, master_weights, adam_m, adam_v)
    owner = lax.axis_index(AXES)
    base_own = lax.dynamic_slice_in_dim(base_weights, owner * rows_dev, rows_dev, 0).astype(
        jnp.float32
    )
    diff_bound = clip_level * jnp.exp2(diff_exps.astype(jnp.float32))
    diff_coded = clip_rows(new_master - base_own, diff_bound).astype(jnp.bfloat16)
    effective = (base_own + diff_coded.astype(jnp.float32)).astype(jnp.bfloat16)
    stacked = gathered(effective, count_z, "z").reshape(count_z * rows_dev, model_width)
    weights = gathered(gathered(stacked, count_y, "second"), count_x, "first")
    peer_part = swapped(project(core_at, peer_tokens, weights, order, count_y))
    own_part = project(core_at, tokens, weights, order, count_y)
    projected = interleaved(core_at, own_part, peer_part)
    return (projected, new_master, new_first, new_second)


def solution(mesh):
    split = Mesh(mesh.devices.reshape(4, 2, 8, 4), AXES)
    rows = P(AXES, None)
    return jax.shard_map(
        shards,
        mesh=split,
        in_specs=(rows, rows, rows, P(), rows, rows, P(AXES, None, None), rows, P()),
        out_specs=(rows, rows, rows, rows),
        check_vma=False,
    )
```

```python
import math

import jax
import jax.numpy as jnp
import numpy as np
from jax import lax
from jax.experimental import pallas as pl
from jax.experimental.pallas import tpu as pltpu
from jax.sharding import Mesh
from jax.sharding import PartitionSpec as P

ADAM_STEP = 10
AXES = ("y", "c", "z", "x")
FACE = ("y", "c", "x")

clip_level = 448.0
beta_one = 0.9
beta_two = 0.95
learn_rate = 0.002
decay_rate = 0.1
adam_eps = 1e-08
highest = lax.Precision.HIGHEST


def hadamard(matrix_size):
    positions = np.arange(matrix_size)
    common = positions[:, None] & positions[None, :]
    parity = np.zeros((matrix_size, matrix_size), np.int32)
    for bit_level in range(matrix_size.bit_length() - 1):
        parity = parity + (common >> bit_level & 1)
    return (1 - 2 * (parity % 2)).astype(np.float32)


def unrotate_rows(row_block, sign_rows, matrix):
    row_count = row_block.shape[0]
    turned = jnp.dot(
        row_block.reshape(-1, sign_rows.shape[1]), matrix, precision=highest
    ) / math.sqrt(sign_rows.shape[1])
    return (turned.reshape(row_count, sign_rows.shape[0], sign_rows.shape[1]) * sign_rows).reshape(
        row_block.shape
    )


def clip_rows(row_block, bound_rows):
    row_count = row_block.shape[0]
    shaped = row_block.reshape(row_count, bound_rows.shape[1], -1)
    limits = bound_rows[:, :, None]
    return jnp.clip(shaped, -limits, limits).reshape(row_block.shape)


def adam_update(gradient, master, first, second):
    new_first = beta_one * first + (1.0 - beta_one) * gradient
    new_second = beta_two * second + (1.0 - beta_two) * gradient * gradient
    fix_one = 1.0 - beta_one**ADAM_STEP
    fix_two = 1.0 - beta_two**ADAM_STEP
    step_dir = new_first / fix_one / (jnp.sqrt(new_second / fix_two) + adam_eps)
    new_master = master - learn_rate * (step_dir + decay_rate * master)
    return (new_master, new_first, new_second)


def row_order(count_z, count_x, rows_dev):
    size = count_z * count_x * rows_dev
    spots = np.arange(size)
    at_x, at_z, at_j = spots // (count_z * rows_dev), spots // rows_dev % count_z, spots % rows_dev
    natural = (at_z * count_x + at_x) * rows_dev + at_j
    return (natural[:, None] == spots[None, :]).astype(np.float32)


def coded_kernel(groups, spots, added, place_ref, tok_ref, *refs):
    grad_refs = refs[:groups]
    sign_ref, exps_ref, mat_ref, order_ref = refs[groups : groups + 4]
    refs = refs[groups + 4 :]
    own_ref = refs[0] if added else None
    out_refs = refs[added:-3]
    turned_ref, grad_t_ref, limit_ref = refs[-3:]
    token_rows, width = tok_ref.shape
    block_len = mat_ref.shape[0]
    tile = order_ref.shape[0]
    part = tile // spots
    core, at_x, at_y = place_ref[0], place_ref[1], place_ref[2]
    first_block = pl.program_id(0) * (width // block_len)

    @pl.when(pl.program_id(0) == 0)
    def _():
        for group in range(groups):
            grad_t = lax.dot_general(
                order_ref[...],
                grad_refs[group][...],
                (((1,), (1,)), ((), ())),
                preferred_element_type=jnp.float32,
            ).astype(jnp.bfloat16)
            from_y = lax.rem(group - at_y + groups, groups)
            for spot in range(spots):
                from_x = lax.rem(spot - at_x + spots, spots)
                piece = jnp.where(core == 0, from_x * groups + from_y, from_y * spots + from_x)
                rows = pl.ds(pl.multiple_of(piece * part, part), part)
                values = grad_t[spot * part : (spot + 1) * part]
                grad_t_ref[rows, :token_rows] = values
                grad_t_ref[rows, token_rows:] = values

    levels = (clip_level * jnp.exp2(exps_ref[...].astype(jnp.float32))).astype(jnp.bfloat16)
    spread_shape = (exps_ref.shape[1], width)
    block_at = lax.broadcasted_iota(jnp.int32, spread_shape, 0) - first_block
    lane_at = lax.broadcasted_iota(jnp.int32, spread_shape, 1)
    start_at = block_at * block_len
    inside = (lane_at >= start_at) & (lane_at < start_at + block_len)
    spread = jnp.where(inside, 1.0, 0.0).astype(jnp.bfloat16)
    limit_ref[...] = jnp.dot(levels, spread, preferred_element_type=jnp.float32)

    scale = 1.0 / math.sqrt(block_len)
    for block in range(width // block_len):
        cols = slice(block * block_len, (block + 1) * block_len)
        signs = 2 * sign_ref[pl.ds(first_block + block, 1), :] - 1
        signed = tok_ref[:, cols] * signs.astype(jnp.float32).astype(jnp.bfloat16)
        turned = jnp.dot(signed, mat_ref[...], preferred_element_type=jnp.float32) * scale
        upper = turned.astype(jnp.bfloat16)
        turned_ref[:token_rows, cols] = upper
        turned_ref[token_rows:, cols] = (turned - upper.astype(jnp.float32)).astype(jnp.bfloat16)
    terms = jnp.dot(grad_t_ref[...], turned_ref[...], preferred_element_type=jnp.float32)
    for first in range(4):
        for second in range(4):
            group = lax.rem(at_y + jnp.where(core == 0, second, first), groups)
            start = (first * 4 + second) * part
            rows = slice(start, start + part)
            limit = limit_ref[pl.ds(2 * group + core, 1), :]
            coded = jnp.clip(terms[rows, :], -limit, limit).astype(jnp.bfloat16)
            if not added:
                out_refs[0][rows, :] = coded
                continue
            total = (coded.astype(jnp.float32) + own_ref[rows, :].astype(jnp.float32)).astype(
                jnp.bfloat16
            )
            if second == 0:
                out_refs[2 * first][...] = total
            else:
                out_refs[2 * first + 1][(second - 1) * part : second * part, :] = total


def coded_gradient(place, tokens, out_grad, signs, exps, matrix, order, own=None):
    token_rows, model_width = tokens.shape
    feature_rows = out_grad.shape[1]
    tile = order.shape[0]
    groups = feature_rows // tile // 2
    spots = 4
    part = tile // spots
    width = 1024
    added = own is not None
    heights = [part, tile - part] * 4 if added else [groups * tile]
    whole = lambda n, place: (0, 0)
    column = lambda n, place: (0, n)
    grad_spec = lambda group: pl.BlockSpec(
        (token_rows, tile), lambda n, place: (0, 2 * group + place[0])
    )
    in_specs = [
        pl.BlockSpec((token_rows, width), column),
        *[grad_spec(group) for group in range(groups)],
        pl.BlockSpec(signs.shape, whole),
        pl.BlockSpec(exps.shape, whole),
        pl.BlockSpec(matrix.shape, whole),
        pl.BlockSpec(order.shape, whole),
    ]
    operands = [tokens, *[out_grad] * groups, signs, exps, matrix, order]
    if added:
        in_specs.append(pl.BlockSpec((groups * tile, width), column))
        operands.append(own)
    body = lambda *refs: coded_kernel(groups, spots, added, *refs)
    return pl.pallas_call(
        body,
        grid_spec=pltpu.PrefetchScalarGridSpec(
            num_scalar_prefetch=1,
            grid=(model_width // width,),
            in_specs=in_specs,
            out_specs=[pl.BlockSpec((height, width), column) for height in heights],
            scratch_shapes=[
                pltpu.VMEM((2 * token_rows, width), jnp.bfloat16),
                pltpu.VMEM((groups * tile, 2 * token_rows), jnp.bfloat16),
                pltpu.VMEM((exps.shape[0], width), jnp.float32),
            ],
        ),
        out_shape=[jax.ShapeDtypeStruct((height, model_width), jnp.bfloat16) for height in heights],
        compiler_params=pltpu.CompilerParams(vmem_limit_bytes=(44 if added else 60) << 20),
    )(place, *operands)


def added_up(refs):
    total = refs[0][...].astype(jnp.float32)
    for ref in refs[1:]:
        total = total + ref[...].astype(jnp.float32)
    return total.astype(jnp.bfloat16)


def line_kernel(count, *refs):
    total = added_up(refs[:count])
    part = refs[count].shape[0]
    for at, out_ref in enumerate(refs[count:]):
        out_ref[...] = total[at * part : (at + 1) * part]


def line_sums(terms, outputs):
    rows, model_width = terms[0].shape
    width = 1024
    spec = lambda height: pl.BlockSpec((height, width), lambda n: (0, n))
    body = lambda *refs: line_kernel(len(terms), *refs)
    return pl.pallas_call(
        body,
        grid=(model_width // width,),
        in_specs=[spec(rows)] * len(terms),
        out_specs=[spec(rows // outputs)] * outputs,
        out_shape=[jax.ShapeDtypeStruct((rows // outputs, model_width), jnp.bfloat16)] * outputs,
        compiler_params=pltpu.CompilerParams(vmem_limit_bytes=16 << 20),
    )(*terms)


def face_kernel(*refs):
    total = added_up(refs[:-1])
    out_ref = refs[-1]
    rows = out_ref.shape[1]
    for at in range(out_ref.shape[0]):
        out_ref[at] = total[at * rows : (at + 1) * rows]


def face_sum(terms, count_z):
    rows, model_width = terms[0].shape
    width = 1024
    return pl.pallas_call(
        face_kernel,
        grid=(model_width // width,),
        in_specs=[pl.BlockSpec((rows, width), lambda n: (0, n))] * len(terms),
        out_specs=pl.BlockSpec((count_z, rows // count_z, width), lambda n: (0, 0, n)),
        out_shape=jax.ShapeDtypeStruct((count_z, rows // count_z, model_width), jnp.bfloat16),
        compiler_params=pltpu.CompilerParams(vmem_limit_bytes=16 << 20),
    )(*terms)


def product(tok_ref, weight_refs):
    weights = jnp.concatenate([ref[...] for ref in weight_refs], axis=0)
    return lax.dot_general(
        weights, tok_ref[...], (((1,), (1,)), ((), ())), preferred_element_type=jnp.float32
    ).astype(jnp.bfloat16)


def early_kernel(tok_ref, *refs):
    refs[-1][...] = product(tok_ref, refs[:-1])


def early_product(tokens, weights):
    whole = pl.BlockSpec(memory_space=pltpu.VMEM)
    rows = sum(value.shape[0] for value in weights)
    return pl.pallas_call(
        early_kernel,
        in_specs=[whole] * (1 + len(weights)),
        out_specs=whole,
        out_shape=jax.ShapeDtypeStruct((rows, tokens.shape[0]), jnp.bfloat16),
        compiler_params=pltpu.CompilerParams(vmem_limit_bytes=24 << 20),
    )(tokens, *weights)


def late_kernel(tok_ref, early_ref, spread_ref, *refs):
    late = product(tok_ref, refs[:-1])
    early_rows = early_ref.shape[0]
    down = (((0,), (0,)), ((), ()))
    out = lax.dot_general(
        early_ref[...], spread_ref[:early_rows, :], down, preferred_element_type=jnp.float32
    )
    out = out + lax.dot_general(
        late, spread_ref[early_rows:, :], down, preferred_element_type=jnp.float32
    )
    refs[-1][...] = out.astype(jnp.bfloat16)


def late_product(tokens, early, spread, weights):
    whole = pl.BlockSpec(memory_space=pltpu.VMEM)
    return pl.pallas_call(
        late_kernel,
        in_specs=[whole] * (3 + len(weights)),
        out_specs=whole,
        out_shape=jax.ShapeDtypeStruct((tokens.shape[0], spread.shape[1]), jnp.bfloat16),
        compiler_params=pltpu.CompilerParams(vmem_limit_bytes=24 << 20),
    )(tokens, early, spread, *weights)


def interleave_kernel(place_ref, own_ref, peer_ref, out_ref):
    tile = 128
    first = place_ref[0] == 0
    for group in range(own_ref.shape[1] // tile):
        cols = slice(group * tile, (group + 1) * tile)
        own, peer = own_ref[:, cols], peer_ref[:, cols]
        start = 2 * group * tile
        out_ref[:, start : start + tile] = jnp.where(first, own, peer)
        out_ref[:, start + tile : start + 2 * tile] = jnp.where(first, peer, own)


def interleaved(place, own_part, peer_part):
    rows, width = own_part.shape
    whole = pl.BlockSpec(memory_space=pltpu.VMEM)
    return pl.pallas_call(
        interleave_kernel,
        in_specs=[pl.BlockSpec(memory_space=pltpu.SMEM), whole, whole],
        out_specs=whole,
        out_shape=jax.ShapeDtypeStruct((rows, 2 * width), jnp.bfloat16),
        compiler_params=pltpu.CompilerParams(vmem_limit_bytes=8 << 20),
    )(place, own_part, peer_part)


def swapped(value):
    return lax.ppermute(value, "c", [(0, 1), (1, 0)])


def shifted(value, axis_at, shift):
    pairs = []
    for y in range(4):
        for core in range(2):
            for x in range(4):
                along_x = core == axis_at
                to_y, to_x = (y, (x + shift) % 4) if along_x else ((y + shift) % 4, x)
                pairs.append(((y * 2 + core) * 4 + x, (to_y * 2 + core) * 4 + to_x))
    return lax.ppermute(value, FACE, pairs)


def column_spread(place, offsets, count_z, rows_dev):
    core, at_x, at_y = place[0], place[1], place[2]
    first = jnp.asarray([offset[0] for offset in offsets], jnp.int32)
    second = jnp.asarray([offset[1] for offset in offsets], jnp.int32)
    from_x = (at_x - jnp.where(core == 0, first, second)) % 4
    from_y = (at_y - jnp.where(core == 0, second, first)) % 4
    at_z = jnp.arange(count_z, dtype=jnp.int32)[None, :, None]
    at_j = jnp.arange(rows_dev, dtype=jnp.int32)[None, None, :]
    column = (
        (from_y[:, None, None] * count_z + at_z) * 4 + from_x[:, None, None]
    ) * rows_dev + at_j
    size = len(offsets) * count_z * rows_dev
    return (column.reshape(size, 1) == jnp.arange(size, dtype=jnp.int32)[None, :]).astype(
        jnp.bfloat16
    )


def shards(
    tokens,
    out_grad,
    master_weights,
    base_weights,
    adam_m,
    adam_v,
    grad_exps,
    diff_exps,
    hadamard_signs,
):
    count_z = lax.axis_size("z")
    rows_dev, model_width = master_weights.shape
    sign_rows = (2 * hadamard_signs - 1).astype(jnp.float32)
    block_len = sign_rows.shape[1]
    matrix = jnp.asarray(hadamard(block_len))
    order = jnp.asarray(row_order(count_z, 4, rows_dev)).astype(jnp.bfloat16)
    half_matrix = matrix.astype(jnp.bfloat16)
    place = jnp.stack([lax.axis_index(axis) for axis in ("c", "x", "y")]).astype(jnp.int32)
    exps = grad_exps[0]
    peer_tokens, peer_grad, peer_exps = swapped(tokens), swapped(out_grad), swapped(exps)
    (own,) = coded_gradient(place, tokens, out_grad, hadamard_signs, exps, half_matrix, order)
    pair_sums = coded_gradient(
        place, peer_tokens, peer_grad, hadamard_signs, peer_exps, half_matrix, order, own=own
    )
    here, far = pair_sums[0::2], pair_sums[1::2]
    arrived = [shifted(far[shift], 0, shift) for shift in (1, 2, 3)]
    lines = line_sums([far[0], *arrived], 3)
    lines, nears = lax.optimization_barrier((list(lines), list(here[1:])))
    crossed = [shifted(lines[shift - 1], 1, shift) for shift in (1, 2, 3)]
    nears = [shifted(nears[shift - 1], 0, shift) for shift in (1, 2, 3)]
    parts = face_sum([here[0], *nears, *crossed], count_z)
    parts = lax.all_to_all(parts, "z", 0, 0, tiled=True)
    summed = jnp.sum(parts.astype(jnp.float32), axis=0)
    gradient = unrotate_rows(summed, sign_rows, matrix)
    new_master, new_first, new_second = adam_update(gradient, master_weights, adam_m, adam_v)
    owner = lax.axis_index(AXES)
    base_own = lax.dynamic_slice_in_dim(base_weights, owner * rows_dev, rows_dev, 0).astype(
        jnp.float32
    )
    diff_bound = clip_level * jnp.exp2(diff_exps.astype(jnp.float32))
    diff_coded = clip_rows(new_master - base_own, diff_bound).astype(jnp.bfloat16)
    effective = (base_own + diff_coded.astype(jnp.float32)).astype(jnp.bfloat16)
    stacked = lax.all_to_all(
        jnp.broadcast_to(effective[None], (count_z, *effective.shape)), "z", 0, 0, tiled=True
    ).reshape(count_z * rows_dev, model_width)
    crossed = [shifted(stacked, 1, shift) for shift in (1, 2, 3)]
    nears = [shifted(stacked, 0, shift) for shift in (1, 2, 3)]
    crossed_rows = jnp.concatenate(crossed, axis=0)
    fars = [shifted(crossed_rows, 0, shift) for shift in (1, 2, 3)]
    offsets = [(0, 0), (1, 0), (2, 0), (3, 0), (0, 1), (0, 2), (0, 3)]
    offsets += [(first, second) for first in (1, 2, 3) for second in (1, 2, 3)]
    spread = column_spread(place, offsets, count_z, rows_dev)
    close = [stacked, *nears, crossed_rows]
    early_own, early_peer = early_product(tokens, close), early_product(peer_tokens, close)
    peer_part = swapped(late_product(peer_tokens, early_peer, spread, fars))
    own_part = late_product(tokens, early_own, spread, fars)
    projected = interleaved(place, own_part, peer_part)
    return (projected, new_master, new_first, new_second)


def solution(mesh):
    split = Mesh(mesh.devices.reshape(4, 2, 8, 4), AXES)
    rows = P(AXES, None)
    return jax.shard_map(
        shards,
        mesh=split,
        in_specs=(rows, rows, rows, P(), rows, rows, P(AXES, None, None), rows, P()),
        out_specs=(rows, rows, rows, rows),
        check_vma=False,
    )
```

```python
import math

import jax
import jax.numpy as jnp
import numpy as np
from jax import lax
from jax.experimental import pallas as pl
from jax.experimental.pallas import tpu as pltpu
from jax.sharding import Mesh
from jax.sharding import PartitionSpec as P

ADAM_STEP = 10
AXES = ("y", "c", "z", "x")
FACE = ("y", "c", "x")

clip_level = 448.0
beta_one = 0.9
beta_two = 0.95
learn_rate = 0.002
decay_rate = 0.1
adam_eps = 1e-08
highest = lax.Precision.HIGHEST


def hadamard(matrix_size):
    positions = np.arange(matrix_size)
    common = positions[:, None] & positions[None, :]
    parity = np.zeros((matrix_size, matrix_size), np.int32)
    for bit_level in range(matrix_size.bit_length() - 1):
        parity = parity + (common >> bit_level & 1)
    return (1 - 2 * (parity % 2)).astype(np.float32)


def unrotate_rows(row_block, sign_rows, matrix):
    row_count = row_block.shape[0]
    turned = jnp.dot(
        row_block.reshape(-1, sign_rows.shape[1]), matrix, precision=highest
    ) / math.sqrt(sign_rows.shape[1])
    return (turned.reshape(row_count, sign_rows.shape[0], sign_rows.shape[1]) * sign_rows).reshape(
        row_block.shape
    )


def clip_rows(row_block, bound_rows):
    row_count = row_block.shape[0]
    shaped = row_block.reshape(row_count, bound_rows.shape[1], -1)
    limits = bound_rows[:, :, None]
    return jnp.clip(shaped, -limits, limits).reshape(row_block.shape)


def adam_update(gradient, master, first, second):
    new_first = beta_one * first + (1.0 - beta_one) * gradient
    new_second = beta_two * second + (1.0 - beta_two) * gradient * gradient
    fix_one = 1.0 - beta_one**ADAM_STEP
    fix_two = 1.0 - beta_two**ADAM_STEP
    step_dir = new_first / fix_one / (jnp.sqrt(new_second / fix_two) + adam_eps)
    new_master = master - learn_rate * (step_dir + decay_rate * master)
    return (new_master, new_first, new_second)


def row_order(count_z, count_x, rows_dev):
    size = count_z * count_x * rows_dev
    spots = np.arange(size)
    at_x, at_z, at_j = spots // (count_z * rows_dev), spots // rows_dev % count_z, spots % rows_dev
    natural = (at_z * count_x + at_x) * rows_dev + at_j
    return (natural[:, None] == spots[None, :]).astype(np.float32)


def coded_kernel(groups, spots, added, offset, core_ref, x_ref, y_ref, tok_ref, *refs):
    grad_refs = refs[:groups]
    sign_ref, exps_ref, mat_ref, order_ref = refs[groups : groups + 4]
    refs = refs[groups + 4 :]
    own_ref = refs[0] if added else None
    out_refs = refs[added:-3]
    turned_ref, grad_t_ref, limit_ref = refs[-3:]
    token_rows, width = tok_ref.shape
    block_len = mat_ref.shape[0]
    tile = order_ref.shape[0]
    part = tile // spots
    core, at_x, at_y = core_ref[0], x_ref[0], y_ref[0]
    first_block = (pl.program_id(0) + offset) * (width // block_len)

    @pl.when(pl.program_id(0) == 0)
    def _():
        for group in range(groups):
            grad_t = lax.dot_general(
                order_ref[...],
                grad_refs[group][...],
                (((1,), (1,)), ((), ())),
                preferred_element_type=jnp.float32,
            ).astype(jnp.bfloat16)
            from_y = lax.rem(group - at_y + groups, groups)
            for spot in range(spots):
                from_x = lax.rem(spot - at_x + spots, spots)
                piece = jnp.where(core == 0, from_x * groups + group, from_y * spots + spot)
                rows = pl.ds(pl.multiple_of(piece * part, part), part)
                values = grad_t[spot * part : (spot + 1) * part]
                grad_t_ref[rows, :token_rows] = values
                grad_t_ref[rows, token_rows:] = values

    levels = (clip_level * jnp.exp2(exps_ref[...].astype(jnp.float32))).astype(jnp.bfloat16)
    spread_shape = (exps_ref.shape[1], width)
    block_at = lax.broadcasted_iota(jnp.int32, spread_shape, 0) - first_block
    lane_at = lax.broadcasted_iota(jnp.int32, spread_shape, 1)
    start_at = block_at * block_len
    inside = (lane_at >= start_at) & (lane_at < start_at + block_len)
    spread = jnp.where(inside, 1.0, 0.0).astype(jnp.bfloat16)
    limit_ref[...] = jnp.dot(levels, spread, preferred_element_type=jnp.float32)

    scale = 1.0 / math.sqrt(block_len)
    for block in range(width // block_len):
        cols = slice(block * block_len, (block + 1) * block_len)
        signs = 2 * sign_ref[pl.ds(first_block + block, 1), :] - 1
        signed = tok_ref[:, cols] * signs.astype(jnp.float32).astype(jnp.bfloat16)
        turned = jnp.dot(signed, mat_ref[...], preferred_element_type=jnp.float32) * scale
        upper = turned.astype(jnp.bfloat16)
        turned_ref[:token_rows, cols] = upper
        turned_ref[token_rows:, cols] = (turned - upper.astype(jnp.float32)).astype(jnp.bfloat16)
    terms = jnp.dot(grad_t_ref[...], turned_ref[...], preferred_element_type=jnp.float32)
    for first in range(4):
        for second in range(4):
            group = jnp.where(core == 0, second, lax.rem(at_y + first, groups))
            start = (first * 4 + second) * part
            rows = slice(start, start + part)
            limit = limit_ref[pl.ds(2 * group + core, 1), :]
            coded = jnp.clip(terms[rows, :], -limit, limit).astype(jnp.bfloat16)
            if not added:
                out_refs[0][rows, :] = coded
                continue
            total = (coded.astype(jnp.float32) + own_ref[rows, :].astype(jnp.float32)).astype(
                jnp.bfloat16
            )
            out_refs[first][second * part : (second + 1) * part, :] = total


def coded_gradient(place, tokens, out_grad, signs, exps, matrix, order, own=None, half=0):
    token_rows, model_width = tokens.shape
    feature_rows = out_grad.shape[1]
    tile = order.shape[0]
    groups = feature_rows // tile // 2
    spots = 4
    width = 1024
    added = own is not None
    heights = [tile] * spots if added else [groups * tile]
    steps = model_width // width // (2 if added else 1)
    offset = half * steps
    whole = lambda n, *place: (0, 0)
    column = lambda n, *place: (0, n + offset)
    placed = lambda n, *place: (0, n)
    grad_spec = lambda group: pl.BlockSpec(
        (token_rows, tile), lambda n, *place: (0, 2 * group + place[0][0])
    )
    in_specs = [
        pl.BlockSpec((token_rows, width), column),
        *[grad_spec(group) for group in range(groups)],
        pl.BlockSpec(signs.shape, whole),
        pl.BlockSpec(exps.shape, whole),
        pl.BlockSpec(matrix.shape, whole),
        pl.BlockSpec(order.shape, whole),
    ]
    operands = [tokens, *[out_grad] * groups, signs, exps, matrix, order]
    if added:
        in_specs.append(pl.BlockSpec((groups * tile, width), column))
        operands.append(own)
    body = lambda *refs: coded_kernel(groups, spots, added, offset, *refs)
    return pl.pallas_call(
        body,
        grid_spec=pltpu.PrefetchScalarGridSpec(
            num_scalar_prefetch=3,
            grid=(steps,),
            in_specs=in_specs,
            out_specs=[pl.BlockSpec((height, width), placed) for height in heights],
            scratch_shapes=[
                pltpu.VMEM((2 * token_rows, width), jnp.bfloat16),
                pltpu.VMEM((groups * tile, 2 * token_rows), jnp.bfloat16),
                pltpu.VMEM((exps.shape[0], width), jnp.float32),
            ],
        ),
        out_shape=[
            jax.ShapeDtypeStruct((height, steps * width), jnp.bfloat16) for height in heights
        ],
        compiler_params=pltpu.CompilerParams(vmem_limit_bytes=(46 if added else 60) << 20),
    )(*place, *operands)


def line_kernel(count, *refs):
    out_ref = refs[-1]
    sums = []
    for terms in (refs[:count], refs[count:-1]):
        total = terms[0][...].astype(jnp.float32)
        for ref in terms[1:]:
            total = total + ref[...].astype(jnp.float32)
        sums.append(total)
    rows = 8
    for at in range(sums[0].shape[0] // rows):
        left, right = (total[at * rows : (at + 1) * rows] for total in sums)
        upper = lax.broadcasted_iota(jnp.int32, left.shape, 0) < rows // 2
        even = jnp.where(upper, left, pltpu.roll(right, rows // 2, 0))
        odd = jnp.where(upper, pltpu.roll(left, rows // 2, 0), right)
        out_ref[2 * at] = even.astype(jnp.bfloat16)
        out_ref[2 * at + 1] = odd.astype(jnp.bfloat16)


def line_sums(left_terms, right_terms):
    rows, half = left_terms[0].shape
    width = 1024
    count = len(left_terms)
    body = lambda *refs: line_kernel(count, *refs)
    return pl.pallas_call(
        body,
        grid=(half // width,),
        in_specs=[pl.BlockSpec((rows, width), lambda n: (0, n))] * (2 * count),
        out_specs=pl.BlockSpec((rows // 4, 8, width), lambda n: (0, 0, n)),
        out_shape=jax.ShapeDtypeStruct((rows // 4, 8, half), jnp.bfloat16),
        compiler_params=pltpu.CompilerParams(vmem_limit_bytes=16 << 20),
    )(*left_terms, *right_terms)


def project_kernel(pair, core_ref, tok_ref, weight_ref, order_ref, out_ref):
    tile = order_ref.shape[0]
    core = core_ref[0]
    rows = []
    for at in range(pair):
        group = pl.program_id(0) * pair + at
        for spot in range(tile // weight_ref.shape[2]):
            first = jnp.where(core == 0, spot, group)
            second = jnp.where(core == 0, group, spot)
            rows.append(weight_ref[first, second])
    total = lax.dot_general(
        tok_ref[...],
        jnp.concatenate(rows, axis=0),
        (((1,), (1,)), ((), ())),
        preferred_element_type=jnp.float32,
    )
    rounded = total.astype(jnp.bfloat16)
    for at in range(pair):
        cols = slice(at * tile, (at + 1) * tile)
        out_ref[:, cols] = jnp.dot(
            rounded[:, cols], order_ref[...], preferred_element_type=jnp.float32
        ).astype(jnp.bfloat16)


def project(core, tokens, weights, order, groups):
    token_rows = tokens.shape[0]
    tile = order.shape[0]
    pair = 2
    body = lambda *refs: project_kernel(pair, *refs)
    return pl.pallas_call(
        body,
        grid_spec=pltpu.PrefetchScalarGridSpec(
            num_scalar_prefetch=1,
            grid=(groups // pair,),
            in_specs=[
                pl.BlockSpec(tokens.shape, lambda n, core: (0, 0)),
                pl.BlockSpec(weights.shape, lambda n, core: (0, 0, 0, 0)),
                pl.BlockSpec(order.shape, lambda n, core: (0, 0)),
            ],
            out_specs=pl.BlockSpec((token_rows, pair * tile), lambda n, core: (0, n)),
        ),
        out_shape=jax.ShapeDtypeStruct((token_rows, groups * tile), jnp.bfloat16),
        compiler_params=pltpu.CompilerParams(vmem_limit_bytes=32 << 20),
    )(core, tokens, weights, order)


def interleave_kernel(core_ref, own_ref, peer_ref, out_ref):
    tile = 128
    first = core_ref[0] == 0
    for group in range(own_ref.shape[1] // tile):
        cols = slice(group * tile, (group + 1) * tile)
        own, peer = own_ref[:, cols], peer_ref[:, cols]
        start = 2 * group * tile
        out_ref[:, start : start + tile] = jnp.where(first, own, peer)
        out_ref[:, start + tile : start + 2 * tile] = jnp.where(first, peer, own)


def interleaved(core, own_part, peer_part):
    rows, width = own_part.shape
    whole = pl.BlockSpec(memory_space=pltpu.VMEM)
    return pl.pallas_call(
        interleave_kernel,
        in_specs=[pl.BlockSpec(memory_space=pltpu.SMEM), whole, whole],
        out_specs=whole,
        out_shape=jax.ShapeDtypeStruct((rows, 2 * width), jnp.bfloat16),
        compiler_params=pltpu.CompilerParams(vmem_limit_bytes=8 << 20),
    )(core, own_part, peer_part)


def swapped(value):
    return lax.ppermute(value, "c", [(0, 1), (1, 0)])


def face_groups(first):
    at = lambda y, c, x: (y * 2 + c) * 4 + x
    groups = []
    for core in (0, 1):
        for line in range(4):
            if (core == 0) == first:
                groups.append([at(line, core, spot) for spot in range(4)])
            else:
                groups.append([at(spot, core, line) for spot in range(4)])
    return groups


def shifted(value, axis_at, shift):
    pairs = []
    for y in range(4):
        for core in range(2):
            for x in range(4):
                along_x = core == axis_at
                to_y, to_x = (y, (x + shift) % 4) if along_x else ((y + shift) % 4, x)
                pairs.append(((y * 2 + core) * 4 + x, (to_y * 2 + core) * 4 + to_x))
    return lax.ppermute(value, FACE, pairs)


def slab_groups():
    at = lambda y, c, z, x: ((y * 2 + c) * 8 + z) * 4 + x
    groups = [[at(y, 0, z, x) for y in range(4) for z in range(8)] for x in range(4)]
    return groups + [[at(y, 1, z, x) for x in range(4) for z in range(8)] for y in range(4)]


def exchanged(value, step):
    if step == "z":
        return lax.all_to_all(value, "z", 0, 0, tiled=True)
    return lax.all_to_all(
        value, FACE, 0, 0, tiled=True, axis_index_groups=face_groups(step == "first")
    )


def gathered(value, count, step):
    return exchanged(jnp.broadcast_to(value[None], (count, *value.shape)), step)


def shards(
    tokens,
    out_grad,
    master_weights,
    base_weights,
    adam_m,
    adam_v,
    grad_exps,
    diff_exps,
    hadamard_signs,
):
    count_y, count_z, count_x = (lax.axis_size(axis) for axis in ("y", "z", "x"))
    rows_dev, model_width = master_weights.shape
    sign_rows = (2 * hadamard_signs - 1).astype(jnp.float32)
    block_len = sign_rows.shape[1]
    matrix = jnp.asarray(hadamard(block_len))
    order = jnp.asarray(row_order(count_z, count_x, rows_dev))
    place = [lax.axis_index(axis).reshape(1).astype(jnp.int32) for axis in ("c", "x", "y")]
    exps = grad_exps[0]
    peer_tokens, peer_grad, peer_exps = swapped(tokens), swapped(out_grad), swapped(exps)
    half_matrix, order = matrix.astype(jnp.bfloat16), order.astype(jnp.bfloat16)
    (own,) = coded_gradient(place, tokens, out_grad, hadamard_signs, exps, half_matrix, order)
    halves = []
    for half in (0, 1):
        pair_sums = coded_gradient(
            place,
            peer_tokens,
            peer_grad,
            hadamard_signs,
            peer_exps,
            half_matrix,
            order,
            own=own,
            half=half,
        )
        halves.append([pair_sums[0], *(shifted(pair_sums[far], 0, far) for far in (2, 1, 3))])
    lines = line_sums(*halves)
    parts = lax.all_to_all(lines, AXES, 0, 0, tiled=True, axis_index_groups=slab_groups())
    summed = jnp.sum(parts.astype(jnp.float32), axis=0)
    summed = jnp.swapaxes(summed.reshape(2, rows_dev, -1), 0, 1).reshape(rows_dev, model_width)
    gradient = unrotate_rows(summed, sign_rows, matrix)
    new_master, new_first, new_second = adam_update(gradient, master_weights, adam_m, adam_v)
    owner = lax.axis_index(AXES)
    base_own = lax.dynamic_slice_in_dim(base_weights, owner * rows_dev, rows_dev, 0).astype(
        jnp.float32
    )
    diff_bound = clip_level * jnp.exp2(diff_exps.astype(jnp.float32))
    diff_coded = clip_rows(new_master - base_own, diff_bound).astype(jnp.bfloat16)
    effective = (base_own + diff_coded.astype(jnp.float32)).astype(jnp.bfloat16)
    stacked = gathered(effective, count_z, "z").reshape(count_z * rows_dev, model_width)
    weights = gathered(gathered(stacked, count_y, "second"), count_x, "first")
    peer_part = swapped(project(place[0], peer_tokens, weights, order, count_y))
    own_part = project(place[0], tokens, weights, order, count_y)
    projected = interleaved(place[0], own_part, peer_part)
    return (projected, new_master, new_first, new_second)


def solution(mesh):
    split = Mesh(mesh.devices.reshape(4, 2, 8, 4), AXES)
    rows = P(AXES, None)
    return jax.shard_map(
        shards,
        mesh=split,
        in_specs=(rows, rows, rows, P(), rows, rows, P(AXES, None, None), rows, P()),
        out_specs=(rows, rows, rows, rows),
        check_vma=False,
    )
```

```python
import math

import jax
import jax.numpy as jnp
import numpy as np
from jax import lax
from jax.experimental import pallas as pl
from jax.experimental.pallas import tpu as pltpu
from jax.sharding import Mesh
from jax.sharding import PartitionSpec as P

ADAM_STEP = 10
AXES = ("y", "c", "z", "x")
FACE = ("y", "c", "x")

clip_level = 448.0
beta_one = 0.9
beta_two = 0.95
learn_rate = 0.002
decay_rate = 0.1
adam_eps = 1e-08
highest = lax.Precision.HIGHEST


def hadamard(matrix_size):
    positions = np.arange(matrix_size)
    common = positions[:, None] & positions[None, :]
    parity = np.zeros((matrix_size, matrix_size), np.int32)
    for bit_level in range(matrix_size.bit_length() - 1):
        parity = parity + (common >> bit_level & 1)
    return (1 - 2 * (parity % 2)).astype(np.float32)


def unrotate_rows(row_block, sign_rows, matrix):
    row_count = row_block.shape[0]
    turned = jnp.dot(
        row_block.reshape(-1, sign_rows.shape[1]), matrix, precision=highest
    ) / math.sqrt(sign_rows.shape[1])
    return (turned.reshape(row_count, sign_rows.shape[0], sign_rows.shape[1]) * sign_rows).reshape(
        row_block.shape
    )


def clip_rows(row_block, bound_rows):
    row_count = row_block.shape[0]
    shaped = row_block.reshape(row_count, bound_rows.shape[1], -1)
    limits = bound_rows[:, :, None]
    return jnp.clip(shaped, -limits, limits).reshape(row_block.shape)


def adam_update(gradient, master, first, second):
    new_first = beta_one * first + (1.0 - beta_one) * gradient
    new_second = beta_two * second + (1.0 - beta_two) * gradient * gradient
    fix_one = 1.0 - beta_one**ADAM_STEP
    fix_two = 1.0 - beta_two**ADAM_STEP
    step_dir = new_first / fix_one / (jnp.sqrt(new_second / fix_two) + adam_eps)
    new_master = master - learn_rate * (step_dir + decay_rate * master)
    return (new_master, new_first, new_second)


def row_order(count_z, count_x, rows_dev):
    size = count_z * count_x * rows_dev
    spots = np.arange(size)
    at_x, at_z, at_j = spots // (count_z * rows_dev), spots // rows_dev % count_z, spots % rows_dev
    natural = (at_z * count_x + at_x) * rows_dev + at_j
    return (natural[:, None] == spots[None, :]).astype(np.float32)


def coded_kernel(groups, spots, added, offset, core_ref, x_ref, y_ref, tok_ref, *refs):
    grad_refs = refs[:groups]
    sign_ref, exps_ref, mat_ref, order_ref = refs[groups : groups + 4]
    refs = refs[groups + 4 :]
    own_ref = refs[0] if added else None
    out_refs = refs[added:-3]
    turned_ref, grad_t_ref, limit_ref = refs[-3:]
    token_rows, width = tok_ref.shape
    block_len = mat_ref.shape[0]
    tile = order_ref.shape[0]
    part = tile // spots
    core, at_x, at_y = core_ref[0], x_ref[0], y_ref[0]
    first_block = (pl.program_id(0) + offset) * (width // block_len)

    @pl.when(pl.program_id(0) == 0)
    def _():
        for group in range(groups):
            grad_t = lax.dot_general(
                order_ref[...],
                grad_refs[group][...],
                (((1,), (1,)), ((), ())),
                preferred_element_type=jnp.float32,
            ).astype(jnp.bfloat16)
            from_y = lax.rem(group - at_y + groups, groups)
            for spot in range(spots):
                from_x = lax.rem(spot - at_x + spots, spots)
                piece = jnp.where(core == 0, from_x * groups + group, from_y * spots + spot)
                rows = pl.ds(pl.multiple_of(piece * part, part), part)
                values = grad_t[spot * part : (spot + 1) * part]
                grad_t_ref[rows, :token_rows] = values
                grad_t_ref[rows, token_rows:] = values

    levels = (clip_level * jnp.exp2(exps_ref[...].astype(jnp.float32))).astype(jnp.bfloat16)
    spread_shape = (exps_ref.shape[1], width)
    block_at = lax.broadcasted_iota(jnp.int32, spread_shape, 0) - first_block
    lane_at = lax.broadcasted_iota(jnp.int32, spread_shape, 1)
    start_at = block_at * block_len
    inside = (lane_at >= start_at) & (lane_at < start_at + block_len)
    spread = jnp.where(inside, 1.0, 0.0).astype(jnp.bfloat16)
    limit_ref[...] = jnp.dot(levels, spread, preferred_element_type=jnp.float32)

    scale = 1.0 / math.sqrt(block_len)
    for block in range(width // block_len):
        cols = slice(block * block_len, (block + 1) * block_len)
        signs = 2 * sign_ref[pl.ds(first_block + block, 1), :] - 1
        signed = tok_ref[:, cols] * signs.astype(jnp.float32).astype(jnp.bfloat16)
        turned = jnp.dot(signed, mat_ref[...], preferred_element_type=jnp.float32) * scale
        upper = turned.astype(jnp.bfloat16)
        turned_ref[:token_rows, cols] = upper
        turned_ref[token_rows:, cols] = (turned - upper.astype(jnp.float32)).astype(jnp.bfloat16)
    terms = jnp.dot(grad_t_ref[...], turned_ref[...], preferred_element_type=jnp.float32)
    for first in range(4):
        for second in range(4):
            group = jnp.where(core == 0, second, lax.rem(at_y + first, groups))
            start = (first * 4 + second) * part
            rows = slice(start, start + part)
            limit = limit_ref[pl.ds(2 * group + core, 1), :]
            coded = jnp.clip(terms[rows, :], -limit, limit).astype(jnp.bfloat16)
            if not added:
                out_refs[0][rows, :] = coded
                continue
            total = (coded.astype(jnp.float32) + own_ref[rows, :].astype(jnp.float32)).astype(
                jnp.bfloat16
            )
            out_refs[first][second * part : (second + 1) * part, :] = total


def coded_gradient(place, tokens, out_grad, signs, exps, matrix, order, own=None, half=0):
    token_rows, model_width = tokens.shape
    feature_rows = out_grad.shape[1]
    tile = order.shape[0]
    groups = feature_rows // tile // 2
    spots = 4
    width = 1024
    added = own is not None
    heights = [tile] * spots if added else [groups * tile]
    steps = model_width // width // (2 if added else 1)
    offset = half * steps
    whole = lambda n, *place: (0, 0)
    column = lambda n, *place: (0, n + offset)
    placed = lambda n, *place: (0, n)
    grad_spec = lambda group: pl.BlockSpec(
        (token_rows, tile), lambda n, *place: (0, 2 * group + place[0][0])
    )
    in_specs = [
        pl.BlockSpec((token_rows, width), column),
        *[grad_spec(group) for group in range(groups)],
        pl.BlockSpec(signs.shape, whole),
        pl.BlockSpec(exps.shape, whole),
        pl.BlockSpec(matrix.shape, whole),
        pl.BlockSpec(order.shape, whole),
    ]
    operands = [tokens, *[out_grad] * groups, signs, exps, matrix, order]
    if added:
        in_specs.append(pl.BlockSpec((groups * tile, width), column))
        operands.append(own)
    body = lambda *refs: coded_kernel(groups, spots, added, offset, *refs)
    return pl.pallas_call(
        body,
        grid_spec=pltpu.PrefetchScalarGridSpec(
            num_scalar_prefetch=3,
            grid=(steps,),
            in_specs=in_specs,
            out_specs=[pl.BlockSpec((height, width), placed) for height in heights],
            scratch_shapes=[
                pltpu.VMEM((2 * token_rows, width), jnp.bfloat16),
                pltpu.VMEM((groups * tile, 2 * token_rows), jnp.bfloat16),
                pltpu.VMEM((exps.shape[0], width), jnp.float32),
            ],
        ),
        out_shape=[
            jax.ShapeDtypeStruct((height, steps * width), jnp.bfloat16) for height in heights
        ],
        compiler_params=pltpu.CompilerParams(vmem_limit_bytes=(46 if added else 60) << 20),
    )(*place, *operands)


def line_kernel(count, *refs):
    out_ref = refs[-1]
    sums = []
    for terms in (refs[:count], refs[count:-1]):
        total = terms[0][...].astype(jnp.float32)
        for ref in terms[1:]:
            total = total + ref[...].astype(jnp.float32)
        sums.append(total)
    rows = 8
    for at in range(sums[0].shape[0] // rows):
        left, right = (total[at * rows : (at + 1) * rows] for total in sums)
        upper = lax.broadcasted_iota(jnp.int32, left.shape, 0) < rows // 2
        even = jnp.where(upper, left, pltpu.roll(right, rows // 2, 0))
        odd = jnp.where(upper, pltpu.roll(left, rows // 2, 0), right)
        out_ref[2 * at] = even.astype(jnp.bfloat16)
        out_ref[2 * at + 1] = odd.astype(jnp.bfloat16)


def line_sums(left_terms, right_terms):
    rows, half = left_terms[0].shape
    width = 1024
    count = len(left_terms)
    body = lambda *refs: line_kernel(count, *refs)
    return pl.pallas_call(
        body,
        grid=(half // width,),
        in_specs=[pl.BlockSpec((rows, width), lambda n: (0, n))] * (2 * count),
        out_specs=pl.BlockSpec((rows // 4, 8, width), lambda n: (0, 0, n)),
        out_shape=jax.ShapeDtypeStruct((rows // 4, 8, half), jnp.bfloat16),
        compiler_params=pltpu.CompilerParams(vmem_limit_bytes=16 << 20),
    )(*left_terms, *right_terms)


def face_kernel(parts_ref, out_ref):
    total = parts_ref[0].astype(jnp.float32)
    for at in range(1, parts_ref.shape[0]):
        total = total + parts_ref[at].astype(jnp.float32)
    out_ref[...] = total.astype(jnp.bfloat16)


def face_sum(parts):
    count, count_z, rows, half = parts.shape
    width = 1024
    return pl.pallas_call(
        face_kernel,
        grid=(half // width,),
        in_specs=[pl.BlockSpec((count, count_z, rows, width), lambda n: (0, 0, 0, n))],
        out_specs=pl.BlockSpec((count_z, rows, width), lambda n: (0, 0, n)),
        out_shape=jax.ShapeDtypeStruct((count_z, rows, half), jnp.bfloat16),
        compiler_params=pltpu.CompilerParams(vmem_limit_bytes=16 << 20),
    )(parts)


def product(tok_ref, weight_refs):
    weights = jnp.concatenate([ref[...] for ref in weight_refs], axis=0)
    return lax.dot_general(
        tok_ref[...], weights, (((1,), (1,)), ((), ())), preferred_element_type=jnp.float32
    ).astype(jnp.bfloat16)


def early_kernel(tok_ref, *refs):
    refs[-1][...] = product(tok_ref, refs[:-1])


def early_product(tokens, weights):
    whole = pl.BlockSpec(memory_space=pltpu.VMEM)
    columns = sum(value.shape[0] for value in weights)
    return pl.pallas_call(
        early_kernel,
        in_specs=[whole] * (1 + len(weights)),
        out_specs=whole,
        out_shape=jax.ShapeDtypeStruct((tokens.shape[0], columns), jnp.bfloat16),
        compiler_params=pltpu.CompilerParams(vmem_limit_bytes=20 << 20),
    )(tokens, *weights)


def late_kernel(count, tok_ref, spread_ref, *refs):
    pieces = [ref[...] for ref in refs[:count]]
    pieces.append(product(tok_ref, refs[count:-1]))
    start, out = 0, None
    for piece in pieces:
        stop = start + piece.shape[1]
        part = jnp.dot(piece, spread_ref[start:stop, :], preferred_element_type=jnp.float32)
        out = part if out is None else out + part
        start = stop
    refs[-1][...] = out.astype(jnp.bfloat16)


def late_product(tokens, spread, done, weights):
    whole = pl.BlockSpec(memory_space=pltpu.VMEM)
    body = lambda *refs: late_kernel(len(done), *refs)
    return pl.pallas_call(
        body,
        in_specs=[whole] * (2 + len(done) + len(weights)),
        out_specs=whole,
        out_shape=jax.ShapeDtypeStruct((tokens.shape[0], spread.shape[1]), jnp.bfloat16),
        compiler_params=pltpu.CompilerParams(vmem_limit_bytes=20 << 20),
    )(tokens, spread, *done, *weights)


def interleave_kernel(core_ref, own_ref, peer_ref, out_ref):
    tile = 128
    first = core_ref[0] == 0
    for group in range(own_ref.shape[1] // tile):
        cols = slice(group * tile, (group + 1) * tile)
        own, peer = own_ref[:, cols], peer_ref[:, cols]
        start = 2 * group * tile
        out_ref[:, start : start + tile] = jnp.where(first, own, peer)
        out_ref[:, start + tile : start + 2 * tile] = jnp.where(first, peer, own)


def interleaved(core, own_part, peer_part):
    rows, width = own_part.shape
    whole = pl.BlockSpec(memory_space=pltpu.VMEM)
    return pl.pallas_call(
        interleave_kernel,
        in_specs=[pl.BlockSpec(memory_space=pltpu.SMEM), whole, whole],
        out_specs=whole,
        out_shape=jax.ShapeDtypeStruct((rows, 2 * width), jnp.bfloat16),
        compiler_params=pltpu.CompilerParams(vmem_limit_bytes=8 << 20),
    )(core, own_part, peer_part)


def swapped(value):
    return lax.ppermute(value, "c", [(0, 1), (1, 0)])


def face_groups(first):
    at = lambda y, c, x: (y * 2 + c) * 4 + x
    groups = []
    for core in (0, 1):
        for line in range(4):
            if (core == 0) == first:
                groups.append([at(line, core, spot) for spot in range(4)])
            else:
                groups.append([at(spot, core, line) for spot in range(4)])
    return groups


def shifted(value, axis_at, shift):
    pairs = []
    for y in range(4):
        for core in range(2):
            for x in range(4):
                along_x = core == axis_at
                to_y, to_x = (y, (x + shift) % 4) if along_x else ((y + shift) % 4, x)
                pairs.append(((y * 2 + core) * 4 + x, (to_y * 2 + core) * 4 + to_x))
    return lax.ppermute(value, FACE, pairs)


def column_spread(place, offsets, count_z, rows_dev):
    core, at_x, at_y = place
    shift = jnp.asarray([offset[0] for offset in offsets], jnp.int32)
    second = jnp.asarray([offset[1] for offset in offsets], jnp.int32)
    from_x = jnp.where(core == 0, (at_x - shift) % 4, second)
    from_y = jnp.where(core == 0, second, (at_y - shift) % 4)
    at_z = jnp.arange(count_z, dtype=jnp.int32)[None, :, None]
    at_j = jnp.arange(rows_dev, dtype=jnp.int32)[None, None, :]
    column = (
        (from_y[:, None, None] * count_z + at_z) * 4 + from_x[:, None, None]
    ) * rows_dev + at_j
    size = len(offsets) * count_z * rows_dev
    return (column.reshape(size, 1) == jnp.arange(size, dtype=jnp.int32)[None, :]).astype(
        jnp.bfloat16
    )


def exchanged(value, step):
    if step == "z":
        return lax.all_to_all(value, "z", 0, 0, tiled=True)
    return lax.all_to_all(
        value, FACE, 0, 0, tiled=True, axis_index_groups=face_groups(step == "first")
    )


def gathered(value, count, step):
    return exchanged(jnp.broadcast_to(value[None], (count, *value.shape)), step)


def shards(
    tokens,
    out_grad,
    master_weights,
    base_weights,
    adam_m,
    adam_v,
    grad_exps,
    diff_exps,
    hadamard_signs,
):
    count_z = lax.axis_size("z")
    rows_dev, model_width = master_weights.shape
    sign_rows = (2 * hadamard_signs - 1).astype(jnp.float32)
    block_len = sign_rows.shape[1]
    matrix = jnp.asarray(hadamard(block_len))
    order = jnp.asarray(row_order(count_z, 4, rows_dev))
    place = [lax.axis_index(axis).reshape(1).astype(jnp.int32) for axis in ("c", "x", "y")]
    exps = grad_exps[0]
    peer_tokens, peer_grad, peer_exps = swapped(tokens), swapped(out_grad), swapped(exps)
    half_matrix, order = matrix.astype(jnp.bfloat16), order.astype(jnp.bfloat16)
    (own,) = coded_gradient(place, tokens, out_grad, hadamard_signs, exps, half_matrix, order)
    halves = []
    for half in (0, 1):
        pair_sums = coded_gradient(
            place,
            peer_tokens,
            peer_grad,
            hadamard_signs,
            peer_exps,
            half_matrix,
            order,
            own=own,
            half=half,
        )
        halves.append([pair_sums[0], *(shifted(pair_sums[far], 0, far) for far in (2, 1, 3))])
    lines = line_sums(*halves)
    lines = exchanged(lines.reshape(4, count_z, 2 * rows_dev, -1), "second")
    parts = exchanged(face_sum(lines), "z")
    summed = jnp.sum(parts.astype(jnp.float32), axis=0)
    summed = jnp.swapaxes(summed.reshape(2, rows_dev, -1), 0, 1).reshape(rows_dev, model_width)
    gradient = unrotate_rows(summed, sign_rows, matrix)
    new_master, new_first, new_second = adam_update(gradient, master_weights, adam_m, adam_v)
    owner = lax.axis_index(AXES)
    base_own = lax.dynamic_slice_in_dim(base_weights, owner * rows_dev, rows_dev, 0).astype(
        jnp.float32
    )
    diff_bound = clip_level * jnp.exp2(diff_exps.astype(jnp.float32))
    diff_coded = clip_rows(new_master - base_own, diff_bound).astype(jnp.bfloat16)
    effective = (base_own + diff_coded.astype(jnp.float32)).astype(jnp.bfloat16)
    stacked = gathered(effective, count_z, "z").reshape(count_z * rows_dev, model_width)
    face = gathered(stacked, 4, "second").reshape(-1, model_width)
    middle = face.shape[0] // 2
    sent = [face[:middle], face[middle:]]
    arrived = [[shifted(rows, 0, far) for far in (2, 1, 3)] for rows in sent]
    offsets = [(0, at) for at in range(4)]
    offsets += [(far, at) for start in (0, 2) for far in (2, 1, 3) for at in (start, start + 1)]
    spread = column_spread(place, offsets, count_z, rows_dev)
    done = [
        [early_product(rows, [face]), early_product(rows, arrived[0])]
        for rows in (tokens, peer_tokens)
    ]
    done, last = lax.optimization_barrier((done, arrived[1]))
    peer_part = swapped(late_product(peer_tokens, spread, done[1], last))
    own_part = late_product(tokens, spread, done[0], last)
    projected = interleaved(place[0], own_part, peer_part)
    return (projected, new_master, new_first, new_second)


def solution(mesh):
    split = Mesh(mesh.devices.reshape(4, 2, 8, 4), AXES)
    rows = P(AXES, None)
    return jax.shard_map(
        shards,
        mesh=split,
        in_specs=(rows, rows, rows, P(), rows, rows, P(AXES, None, None), rows, P()),
        out_specs=(rows, rows, rows, rows),
        check_vma=False,
    )
```

```python
import math

import jax
import jax.numpy as jnp
import numpy as np
from jax import lax
from jax.experimental import pallas as pl
from jax.experimental.pallas import tpu as pltpu
from jax.sharding import Mesh
from jax.sharding import PartitionSpec as P

ADAM_STEP = 10
AXES = ("y", "c", "z", "x")
FACE = ("y", "c", "x")

clip_level = 448.0
beta_one = 0.9
beta_two = 0.95
learn_rate = 0.002
decay_rate = 0.1
adam_eps = 1e-08
highest = lax.Precision.HIGHEST


def hadamard(matrix_size):
    positions = np.arange(matrix_size)
    common = positions[:, None] & positions[None, :]
    parity = np.zeros((matrix_size, matrix_size), np.int32)
    for bit_level in range(matrix_size.bit_length() - 1):
        parity = parity + (common >> bit_level & 1)
    return (1 - 2 * (parity % 2)).astype(np.float32)


def unrotate_rows(row_block, sign_rows, matrix):
    row_count = row_block.shape[0]
    turned = jnp.dot(
        row_block.reshape(-1, sign_rows.shape[1]), matrix, precision=highest
    ) / math.sqrt(sign_rows.shape[1])
    return (turned.reshape(row_count, sign_rows.shape[0], sign_rows.shape[1]) * sign_rows).reshape(
        row_block.shape
    )


def clip_rows(row_block, bound_rows):
    row_count = row_block.shape[0]
    shaped = row_block.reshape(row_count, bound_rows.shape[1], -1)
    limits = bound_rows[:, :, None]
    return jnp.clip(shaped, -limits, limits).reshape(row_block.shape)


def adam_update(gradient, master, first, second):
    new_first = beta_one * first + (1.0 - beta_one) * gradient
    new_second = beta_two * second + (1.0 - beta_two) * gradient * gradient
    fix_one = 1.0 - beta_one**ADAM_STEP
    fix_two = 1.0 - beta_two**ADAM_STEP
    step_dir = new_first / fix_one / (jnp.sqrt(new_second / fix_two) + adam_eps)
    new_master = master - learn_rate * (step_dir + decay_rate * master)
    return (new_master, new_first, new_second)


def row_order(count_z, count_x, rows_dev):
    size = count_z * count_x * rows_dev
    spots = np.arange(size)
    at_x, at_z, at_j = spots // (count_z * rows_dev), spots // rows_dev % count_z, spots % rows_dev
    natural = (at_z * count_x + at_x) * rows_dev + at_j
    return (natural[:, None] == spots[None, :]).astype(np.float32)


def coded_kernel(groups, spots, added, offset, core_ref, x_ref, y_ref, tok_ref, *refs):
    grad_refs = refs[:groups]
    sign_ref, exps_ref, mat_ref, order_ref = refs[groups : groups + 4]
    refs = refs[groups + 4 :]
    own_ref = refs[0] if added else None
    out_refs = refs[added:-3]
    turned_ref, grad_t_ref, limit_ref = refs[-3:]
    token_rows, width = tok_ref.shape
    block_len = mat_ref.shape[0]
    tile = order_ref.shape[0]
    part = tile // spots
    core, at_x, at_y = core_ref[0], x_ref[0], y_ref[0]
    first_block = (pl.program_id(0) + offset) * (width // block_len)

    @pl.when(pl.program_id(0) == 0)
    def _():
        for group in range(groups):
            grad_t = lax.dot_general(
                order_ref[...],
                grad_refs[group][...],
                (((1,), (1,)), ((), ())),
                preferred_element_type=jnp.float32,
            ).astype(jnp.bfloat16)
            from_y = lax.rem(group - at_y + groups, groups)
            for spot in range(spots):
                from_x = lax.rem(spot - at_x + spots, spots)
                piece = jnp.where(core == 0, from_x * groups + group, from_y * spots + spot)
                rows = pl.ds(pl.multiple_of(piece * part, part), part)
                values = grad_t[spot * part : (spot + 1) * part]
                grad_t_ref[rows, :token_rows] = values
                grad_t_ref[rows, token_rows:] = values

    levels = (clip_level * jnp.exp2(exps_ref[...].astype(jnp.float32))).astype(jnp.bfloat16)
    spread_shape = (exps_ref.shape[1], width)
    block_at = lax.broadcasted_iota(jnp.int32, spread_shape, 0) - first_block
    lane_at = lax.broadcasted_iota(jnp.int32, spread_shape, 1)
    start_at = block_at * block_len
    inside = (lane_at >= start_at) & (lane_at < start_at + block_len)
    spread = jnp.where(inside, 1.0, 0.0).astype(jnp.bfloat16)
    limit_ref[...] = jnp.dot(levels, spread, preferred_element_type=jnp.float32)

    scale = 1.0 / math.sqrt(block_len)
    for block in range(width // block_len):
        cols = slice(block * block_len, (block + 1) * block_len)
        signs = 2 * sign_ref[pl.ds(first_block + block, 1), :] - 1
        signed = tok_ref[:, cols] * signs.astype(jnp.float32).astype(jnp.bfloat16)
        turned = jnp.dot(signed, mat_ref[...], preferred_element_type=jnp.float32) * scale
        upper = turned.astype(jnp.bfloat16)
        turned_ref[:token_rows, cols] = upper
        turned_ref[token_rows:, cols] = (turned - upper.astype(jnp.float32)).astype(jnp.bfloat16)
    terms = jnp.dot(grad_t_ref[...], turned_ref[...], preferred_element_type=jnp.float32)
    for first in range(4):
        for second in range(4):
            group = jnp.where(core == 0, second, lax.rem(at_y + first, groups))
            start = (first * 4 + second) * part
            rows = slice(start, start + part)
            limit = limit_ref[pl.ds(2 * group + core, 1), :]
            coded = jnp.clip(terms[rows, :], -limit, limit).astype(jnp.bfloat16)
            if not added:
                out_refs[0][rows, :] = coded
                continue
            total = (coded.astype(jnp.float32) + own_ref[rows, :].astype(jnp.float32)).astype(
                jnp.bfloat16
            )
            out_refs[first][second * part : (second + 1) * part, :] = total


def coded_gradient(place, tokens, out_grad, signs, exps, matrix, order, own=None, half=0):
    token_rows, model_width = tokens.shape
    feature_rows = out_grad.shape[1]
    tile = order.shape[0]
    groups = feature_rows // tile // 2
    spots = 4
    width = 1024
    added = own is not None
    heights = [tile] * spots if added else [groups * tile]
    steps = model_width // width // (2 if added else 1)
    offset = half * steps
    whole = lambda n, *place: (0, 0)
    column = lambda n, *place: (0, n + offset)
    placed = lambda n, *place: (0, n)
    grad_spec = lambda group: pl.BlockSpec(
        (token_rows, tile), lambda n, *place: (0, 2 * group + place[0][0])
    )
    in_specs = [
        pl.BlockSpec((token_rows, width), column),
        *[grad_spec(group) for group in range(groups)],
        pl.BlockSpec(signs.shape, whole),
        pl.BlockSpec(exps.shape, whole),
        pl.BlockSpec(matrix.shape, whole),
        pl.BlockSpec(order.shape, whole),
    ]
    operands = [tokens, *[out_grad] * groups, signs, exps, matrix, order]
    if added:
        in_specs.append(pl.BlockSpec((groups * tile, width), column))
        operands.append(own)
    body = lambda *refs: coded_kernel(groups, spots, added, offset, *refs)
    return pl.pallas_call(
        body,
        grid_spec=pltpu.PrefetchScalarGridSpec(
            num_scalar_prefetch=3,
            grid=(steps,),
            in_specs=in_specs,
            out_specs=[pl.BlockSpec((height, width), placed) for height in heights],
            scratch_shapes=[
                pltpu.VMEM((2 * token_rows, width), jnp.bfloat16),
                pltpu.VMEM((groups * tile, 2 * token_rows), jnp.bfloat16),
                pltpu.VMEM((exps.shape[0], width), jnp.float32),
            ],
        ),
        out_shape=[
            jax.ShapeDtypeStruct((height, steps * width), jnp.bfloat16) for height in heights
        ],
        compiler_params=pltpu.CompilerParams(vmem_limit_bytes=(46 if added else 60) << 20),
    )(*place, *operands)


def added_up(refs):
    total = refs[0][...].astype(jnp.float32)
    for ref in refs[1:]:
        total = total + ref[...].astype(jnp.float32)
    return total


def line_kernel(*refs):
    refs[-1][...] = added_up(refs[:-1]).astype(jnp.bfloat16)


def line_sum(terms):
    rows, half = terms[0].shape
    width = 1024
    spec = pl.BlockSpec((rows, width), lambda n: (0, n))
    return pl.pallas_call(
        line_kernel,
        grid=(half // width,),
        in_specs=[spec] * len(terms),
        out_specs=spec,
        out_shape=jax.ShapeDtypeStruct((rows, half), jnp.bfloat16),
        compiler_params=pltpu.CompilerParams(vmem_limit_bytes=16 << 20),
    )(*terms)


def face_kernel(left_ref, right_ref, out_ref):
    left_sum, right_sum = (
        added_up([ref.at[at] for at in range(ref.shape[0])]) for ref in (left_ref, right_ref)
    )
    rows = 8
    for at in range(left_sum.shape[0] // rows):
        left, right = (total[at * rows : (at + 1) * rows] for total in (left_sum, right_sum))
        upper = lax.broadcasted_iota(jnp.int32, left.shape, 0) < rows // 2
        even = jnp.where(upper, left, pltpu.roll(right, rows // 2, 0))
        odd = jnp.where(upper, pltpu.roll(left, rows // 2, 0), right)
        out_ref[2 * at] = even.astype(jnp.bfloat16)
        out_ref[2 * at + 1] = odd.astype(jnp.bfloat16)


def face_sum(left, right):
    count, rows, half = left.shape
    width = 1024
    return pl.pallas_call(
        face_kernel,
        grid=(half // width,),
        in_specs=[pl.BlockSpec((count, rows, width), lambda n: (0, 0, n))] * 2,
        out_specs=pl.BlockSpec((rows // 4, 8, width), lambda n: (0, 0, n)),
        out_shape=jax.ShapeDtypeStruct((rows // 4, 8, half), jnp.bfloat16),
        compiler_params=pltpu.CompilerParams(vmem_limit_bytes=16 << 20),
    )(left, right)


def product(tok_ref, weight_refs):
    weights = jnp.concatenate([ref[...] for ref in weight_refs], axis=0)
    return lax.dot_general(
        tok_ref[...], weights, (((1,), (1,)), ((), ())), preferred_element_type=jnp.float32
    ).astype(jnp.bfloat16)


def early_kernel(tok_ref, spread_ref, *refs):
    refs[-1][...] = jnp.dot(
        product(tok_ref, refs[:-1]), spread_ref[...], preferred_element_type=jnp.float32
    ).astype(jnp.bfloat16)


def early_product(tokens, spread, weights):
    whole = pl.BlockSpec(memory_space=pltpu.VMEM)
    return pl.pallas_call(
        early_kernel,
        in_specs=[whole] * (2 + len(weights)),
        out_specs=whole,
        out_shape=jax.ShapeDtypeStruct((tokens.shape[0], spread.shape[1]), jnp.bfloat16),
        compiler_params=pltpu.CompilerParams(vmem_limit_bytes=20 << 20),
    )(tokens, spread, *weights)


def late_kernel(tok_ref, spread_ref, early_ref, *refs):
    late = jnp.dot(
        product(tok_ref, refs[:-1]), spread_ref[...], preferred_element_type=jnp.float32
    )
    refs[-1][...] = (late + early_ref[...].astype(jnp.float32)).astype(jnp.bfloat16)


def late_product(tokens, spread, early, weights):
    whole = pl.BlockSpec(memory_space=pltpu.VMEM)
    return pl.pallas_call(
        late_kernel,
        in_specs=[whole] * (3 + len(weights)),
        out_specs=whole,
        out_shape=jax.ShapeDtypeStruct((tokens.shape[0], spread.shape[1]), jnp.bfloat16),
        compiler_params=pltpu.CompilerParams(vmem_limit_bytes=20 << 20),
    )(tokens, spread, early, *weights)


def interleave_kernel(core_ref, own_ref, peer_ref, out_ref):
    tile = 128
    first = core_ref[0] == 0
    for group in range(own_ref.shape[1] // tile):
        cols = slice(group * tile, (group + 1) * tile)
        own, peer = own_ref[:, cols], peer_ref[:, cols]
        start = 2 * group * tile
        out_ref[:, start : start + tile] = jnp.where(first, own, peer)
        out_ref[:, start + tile : start + 2 * tile] = jnp.where(first, peer, own)


def interleaved(core, own_part, peer_part):
    rows, width = own_part.shape
    whole = pl.BlockSpec(memory_space=pltpu.VMEM)
    return pl.pallas_call(
        interleave_kernel,
        in_specs=[pl.BlockSpec(memory_space=pltpu.SMEM), whole, whole],
        out_specs=whole,
        out_shape=jax.ShapeDtypeStruct((rows, 2 * width), jnp.bfloat16),
        compiler_params=pltpu.CompilerParams(vmem_limit_bytes=8 << 20),
    )(core, own_part, peer_part)


def swapped(value):
    return lax.ppermute(value, "c", [(0, 1), (1, 0)])


def face_groups(first):
    at = lambda y, c, x: (y * 2 + c) * 4 + x
    groups = []
    for core in (0, 1):
        for line in range(4):
            if (core == 0) == first:
                groups.append([at(line, core, spot) for spot in range(4)])
            else:
                groups.append([at(spot, core, line) for spot in range(4)])
    return groups


def shifted(value, axis_at, shift):
    pairs = []
    for y in range(4):
        for core in range(2):
            for x in range(4):
                along_x = core == axis_at
                to_y, to_x = (y, (x + shift) % 4) if along_x else ((y + shift) % 4, x)
                pairs.append(((y * 2 + core) * 4 + x, (to_y * 2 + core) * 4 + to_x))
    return lax.ppermute(value, FACE, pairs)


def column_spread(place, pieces, count_z, rows_dev):
    core, at_x, at_y = place
    shift = jnp.asarray([piece[0] for piece in pieces], jnp.int32)[:, None, None, None]
    start = jnp.asarray([piece[1] for piece in pieces], jnp.int32)[:, None, None, None]
    second = jnp.arange(4, dtype=jnp.int32)[None, :, None, None]
    at_z = jnp.arange(count_z // 2, dtype=jnp.int32)[None, None, :, None] + start
    at_j = jnp.arange(rows_dev, dtype=jnp.int32)[None, None, None, :]
    from_x = jnp.where(core == 0, (at_x - shift) % 4, second)
    from_y = jnp.where(core == 0, second, (at_y - shift) % 4)
    column = ((from_y * count_z + at_z) * 4 + from_x) * rows_dev + at_j
    size = 16 * count_z * rows_dev
    return (column.reshape(-1, 1) == jnp.arange(size, dtype=jnp.int32)[None, :]).astype(
        jnp.bfloat16
    )


def exchanged(value, step):
    if step == "z":
        return lax.all_to_all(value, "z", 0, 0, tiled=True)
    return lax.all_to_all(
        value, FACE, 0, 0, tiled=True, axis_index_groups=face_groups(step == "first")
    )


def gathered(value, count, step):
    return exchanged(jnp.broadcast_to(value[None], (count, *value.shape)), step)


def shards(
    tokens,
    out_grad,
    master_weights,
    base_weights,
    adam_m,
    adam_v,
    grad_exps,
    diff_exps,
    hadamard_signs,
):
    count_z = lax.axis_size("z")
    rows_dev, model_width = master_weights.shape
    sign_rows = (2 * hadamard_signs - 1).astype(jnp.float32)
    block_len = sign_rows.shape[1]
    matrix = jnp.asarray(hadamard(block_len))
    order = jnp.asarray(row_order(count_z, 4, rows_dev))
    place = [lax.axis_index(axis).reshape(1).astype(jnp.int32) for axis in ("c", "x", "y")]
    exps = grad_exps[0]
    peer_tokens, peer_grad, peer_exps = swapped(tokens), swapped(out_grad), swapped(exps)
    half_matrix, order = matrix.astype(jnp.bfloat16), order.astype(jnp.bfloat16)
    (own,) = coded_gradient(place, tokens, out_grad, hadamard_signs, exps, half_matrix, order)
    halves = []
    for half in (0, 1):
        pair_sums = coded_gradient(
            place,
            peer_tokens,
            peer_grad,
            hadamard_signs,
            peer_exps,
            half_matrix,
            order,
            own=own,
            half=half,
        )
        halves.append([pair_sums[0], *(shifted(pair_sums[far], 0, far) for far in (2, 1, 3))])
    lines = [line_sum(terms).reshape(4, -1, terms[0].shape[1]) for terms in halves]
    parts = exchanged(face_sum(*(exchanged(rows, "second") for rows in lines)), "z")
    summed = jnp.sum(parts.astype(jnp.float32), axis=0)
    summed = jnp.swapaxes(summed.reshape(2, rows_dev, -1), 0, 1).reshape(rows_dev, model_width)
    gradient = unrotate_rows(summed, sign_rows, matrix)
    new_master, new_first, new_second = adam_update(gradient, master_weights, adam_m, adam_v)
    owner = lax.axis_index(AXES)
    base_own = lax.dynamic_slice_in_dim(base_weights, owner * rows_dev, rows_dev, 0).astype(
        jnp.float32
    )
    diff_bound = clip_level * jnp.exp2(diff_exps.astype(jnp.float32))
    diff_coded = clip_rows(new_master - base_own, diff_bound).astype(jnp.bfloat16)
    effective = (base_own + diff_coded.astype(jnp.float32)).astype(jnp.bfloat16)
    stacked = gathered(effective, count_z, "z").reshape(count_z * rows_dev, model_width)
    middle = stacked.shape[0] // 2
    faces, arrived = [], []
    for rows in (stacked[:middle], stacked[middle:]):
        faces.append(gathered(rows, 4, "second").reshape(-1, model_width))
        arrived.append([shifted(faces[-1], 0, far) for far in (2, 1, 3)])
    first_z = (0, count_z // 2)
    early_pieces = [(0, first_z[0]), *((far, first_z[0]) for far in (2, 1, 3)), (0, first_z[1])]
    early_spread = column_spread(place, early_pieces, count_z, rows_dev)
    late_spread = column_spread(
        place, [(far, first_z[1]) for far in (2, 1, 3)], count_z, rows_dev
    )
    near = [faces[0], *arrived[0], faces[1]]
    early = [early_product(rows, early_spread, near) for rows in (peer_tokens, tokens)]
    early, last = lax.optimization_barrier((early, arrived[1]))
    peer_part = swapped(late_product(peer_tokens, late_spread, early[0], last))
    own_part = late_product(tokens, late_spread, early[1], last)
    projected = interleaved(place[0], own_part, peer_part)
    return (projected, new_master, new_first, new_second)


def solution(mesh):
    split = Mesh(mesh.devices.reshape(4, 2, 8, 4), AXES)
    rows = P(AXES, None)
    return jax.shard_map(
        shards,
        mesh=split,
        in_specs=(rows, rows, rows, P(), rows, rows, P(AXES, None, None), rows, P()),
        out_specs=(rows, rows, rows, rows),
        check_vma=False,
    )
```

```python
import math

import jax
import jax.numpy as jnp
import numpy as np
from jax import lax
from jax.experimental import pallas as pl
from jax.experimental.pallas import tpu as pltpu
from jax.sharding import Mesh
from jax.sharding import PartitionSpec as P

ADAM_STEP = 10
AXES = ("y", "c", "z", "x")
FACE = ("y", "c", "x")

clip_level = 448.0
beta_one = 0.9
beta_two = 0.95
learn_rate = 0.002
decay_rate = 0.1
adam_eps = 1e-08
highest = lax.Precision.HIGHEST


def hadamard(matrix_size):
    positions = np.arange(matrix_size)
    common = positions[:, None] & positions[None, :]
    parity = np.zeros((matrix_size, matrix_size), np.int32)
    for bit_level in range(matrix_size.bit_length() - 1):
        parity = parity + (common >> bit_level & 1)
    return (1 - 2 * (parity % 2)).astype(np.float32)


def unrotate_rows(row_block, sign_rows, matrix):
    row_count = row_block.shape[0]
    turned = jnp.dot(
        row_block.reshape(-1, sign_rows.shape[1]), matrix, precision=highest
    ) / math.sqrt(sign_rows.shape[1])
    return (turned.reshape(row_count, sign_rows.shape[0], sign_rows.shape[1]) * sign_rows).reshape(
        row_block.shape
    )


def clip_rows(row_block, bound_rows):
    row_count = row_block.shape[0]
    shaped = row_block.reshape(row_count, bound_rows.shape[1], -1)
    limits = bound_rows[:, :, None]
    return jnp.clip(shaped, -limits, limits).reshape(row_block.shape)


def adam_update(gradient, master, first, second):
    new_first = beta_one * first + (1.0 - beta_one) * gradient
    new_second = beta_two * second + (1.0 - beta_two) * gradient * gradient
    fix_one = 1.0 - beta_one**ADAM_STEP
    fix_two = 1.0 - beta_two**ADAM_STEP
    step_dir = new_first / fix_one / (jnp.sqrt(new_second / fix_two) + adam_eps)
    new_master = master - learn_rate * (step_dir + decay_rate * master)
    return (new_master, new_first, new_second)


def row_order(count_z, count_x, rows_dev):
    size = count_z * count_x * rows_dev
    spots = np.arange(size)
    at_x, at_z, at_j = spots // (count_z * rows_dev), spots // rows_dev % count_z, spots % rows_dev
    natural = (at_z * count_x + at_x) * rows_dev + at_j
    return (natural[:, None] == spots[None, :]).astype(np.float32)


def coded_kernel(groups, spots, added, offset, core_ref, x_ref, y_ref, tok_ref, *refs):
    grad_refs = refs[:groups]
    sign_ref, exps_ref, mat_ref, order_ref = refs[groups : groups + 4]
    refs = refs[groups + 4 :]
    own_ref = refs[0] if added else None
    out_refs = refs[added:-3]
    turned_ref, grad_t_ref, limit_ref = refs[-3:]
    token_rows, width = tok_ref.shape
    block_len = mat_ref.shape[0]
    tile = order_ref.shape[0]
    part = tile // spots
    core, at_x, at_y = core_ref[0], x_ref[0], y_ref[0]
    first_block = (pl.program_id(0) + offset) * (width // block_len)

    @pl.when(pl.program_id(0) == 0)
    def _():
        for group in range(groups):
            grad_t = lax.dot_general(
                order_ref[...],
                grad_refs[group][...],
                (((1,), (1,)), ((), ())),
                preferred_element_type=jnp.float32,
            ).astype(jnp.bfloat16)
            from_y = lax.rem(group - at_y + groups, groups)
            for spot in range(spots):
                from_x = lax.rem(spot - at_x + spots, spots)
                piece = jnp.where(core == 0, from_x * groups + from_y, from_y * spots + from_x)
                rows = pl.ds(pl.multiple_of(piece * part, part), part)
                values = grad_t[spot * part : (spot + 1) * part]
                grad_t_ref[rows, :token_rows] = values
                grad_t_ref[rows, token_rows:] = values

    levels = (clip_level * jnp.exp2(exps_ref[...].astype(jnp.float32))).astype(jnp.bfloat16)
    spread_shape = (exps_ref.shape[1], width)
    block_at = lax.broadcasted_iota(jnp.int32, spread_shape, 0) - first_block
    lane_at = lax.broadcasted_iota(jnp.int32, spread_shape, 1)
    start_at = block_at * block_len
    inside = (lane_at >= start_at) & (lane_at < start_at + block_len)
    spread = jnp.where(inside, 1.0, 0.0).astype(jnp.bfloat16)
    limit_ref[...] = jnp.dot(levels, spread, preferred_element_type=jnp.float32)

    scale = 1.0 / math.sqrt(block_len)
    for block in range(width // block_len):
        cols = slice(block * block_len, (block + 1) * block_len)
        signs = 2 * sign_ref[pl.ds(first_block + block, 1), :] - 1
        signed = tok_ref[:, cols] * signs.astype(jnp.float32).astype(jnp.bfloat16)
        turned = jnp.dot(signed, mat_ref[...], preferred_element_type=jnp.float32) * scale
        upper = turned.astype(jnp.bfloat16)
        turned_ref[:token_rows, cols] = upper
        turned_ref[token_rows:, cols] = (turned - upper.astype(jnp.float32)).astype(jnp.bfloat16)
    terms = jnp.dot(grad_t_ref[...], turned_ref[...], preferred_element_type=jnp.float32)
    for first in range(4):
        for second in range(4):
            group = lax.rem(at_y + jnp.where(core == 0, second, first), groups)
            start = (first * 4 + second) * part
            rows = slice(start, start + part)
            limit = limit_ref[pl.ds(2 * group + core, 1), :]
            coded = jnp.clip(terms[rows, :], -limit, limit).astype(jnp.bfloat16)
            if not added:
                out_refs[0][rows, :] = coded
                continue
            total = (coded.astype(jnp.float32) + own_ref[rows, :].astype(jnp.float32)).astype(
                jnp.bfloat16
            )
            out_refs[first][second * part : (second + 1) * part, :] = total


def coded_gradient(place, tokens, out_grad, signs, exps, matrix, order, own=None, half=0):
    token_rows, model_width = tokens.shape
    feature_rows = out_grad.shape[1]
    tile = order.shape[0]
    groups = feature_rows // tile // 2
    spots = 4
    width = 1024
    added = own is not None
    heights = [tile] * spots if added else [groups * tile]
    steps = model_width // width // (2 if added else 1)
    offset = half * steps
    whole = lambda n, *place: (0, 0)
    column = lambda n, *place: (0, n + offset)
    placed = lambda n, *place: (0, n)
    grad_spec = lambda group: pl.BlockSpec(
        (token_rows, tile), lambda n, *place: (0, 2 * group + place[0][0])
    )
    in_specs = [
        pl.BlockSpec((token_rows, width), column),
        *[grad_spec(group) for group in range(groups)],
        pl.BlockSpec(signs.shape, whole),
        pl.BlockSpec(exps.shape, whole),
        pl.BlockSpec(matrix.shape, whole),
        pl.BlockSpec(order.shape, whole),
    ]
    operands = [tokens, *[out_grad] * groups, signs, exps, matrix, order]
    if added:
        in_specs.append(pl.BlockSpec((groups * tile, width), column))
        operands.append(own)
    body = lambda *refs: coded_kernel(groups, spots, added, offset, *refs)
    return pl.pallas_call(
        body,
        grid_spec=pltpu.PrefetchScalarGridSpec(
            num_scalar_prefetch=3,
            grid=(steps,),
            in_specs=in_specs,
            out_specs=[pl.BlockSpec((height, width), placed) for height in heights],
            scratch_shapes=[
                pltpu.VMEM((2 * token_rows, width), jnp.bfloat16),
                pltpu.VMEM((groups * tile, 2 * token_rows), jnp.bfloat16),
                pltpu.VMEM((exps.shape[0], width), jnp.float32),
            ],
        ),
        out_shape=[
            jax.ShapeDtypeStruct((height, steps * width), jnp.bfloat16) for height in heights
        ],
        compiler_params=pltpu.CompilerParams(vmem_limit_bytes=(46 if added else 60) << 20),
    )(*place, *operands)


def added_up(refs):
    total = refs[0][...].astype(jnp.float32)
    for ref in refs[1:]:
        total = total + ref[...].astype(jnp.float32)
    return total


def line_kernel(count, *refs):
    out_refs = refs[2 * count :]
    sums = added_up(refs[:count]), added_up(refs[count : 2 * count])
    rows = 8
    pairs = sums[0].shape[0] // rows // len(out_refs)
    for at in range(sums[0].shape[0] // rows):
        left, right = (total[at * rows : (at + 1) * rows] for total in sums)
        upper = lax.broadcasted_iota(jnp.int32, left.shape, 0) < rows // 2
        even = jnp.where(upper, left, pltpu.roll(right, rows // 2, 0))
        odd = jnp.where(upper, pltpu.roll(left, rows // 2, 0), right)
        out_refs[at // pairs][2 * (at % pairs)] = even.astype(jnp.bfloat16)
        out_refs[at // pairs][2 * (at % pairs) + 1] = odd.astype(jnp.bfloat16)


def line_sums(left_terms, right_terms):
    rows, half = left_terms[0].shape
    width = 1024
    count = len(left_terms)
    shape = (rows // 16, 8, half)
    body = lambda *refs: line_kernel(count, *refs)
    return pl.pallas_call(
        body,
        grid=(half // width,),
        in_specs=[pl.BlockSpec((rows, width), lambda n: (0, n))] * (2 * count),
        out_specs=[pl.BlockSpec((*shape[:2], width), lambda n: (0, 0, n))] * 4,
        out_shape=[jax.ShapeDtypeStruct(shape, jnp.bfloat16)] * 4,
        compiler_params=pltpu.CompilerParams(vmem_limit_bytes=16 << 20),
    )(*left_terms, *right_terms)


def face_kernel(*refs):
    refs[-1][...] = added_up(refs[:-1]).astype(jnp.bfloat16)


def face_sum(terms):
    count_z, rows, half = terms[0].shape
    width = 1024
    spec = pl.BlockSpec((count_z, rows, width), lambda n: (0, 0, n))
    return pl.pallas_call(
        face_kernel,
        grid=(half // width,),
        in_specs=[spec] * len(terms),
        out_specs=spec,
        out_shape=jax.ShapeDtypeStruct(terms[0].shape, jnp.bfloat16),
        compiler_params=pltpu.CompilerParams(vmem_limit_bytes=16 << 20),
    )(*terms)


def pack_kernel(*refs):
    rows = refs[0].shape[0]
    for at, ref in enumerate(refs[:-1]):
        refs[-1][at * rows : (at + 1) * rows, :] = ref[...]


def packed(pieces):
    rows, model_width = pieces[0].shape
    whole = pl.BlockSpec(memory_space=pltpu.VMEM)
    return pl.pallas_call(
        pack_kernel,
        in_specs=[whole] * len(pieces),
        out_specs=whole,
        out_shape=jax.ShapeDtypeStruct((len(pieces) * rows, model_width), jnp.bfloat16),
        compiler_params=pltpu.CompilerParams(vmem_limit_bytes=8 << 20),
    )(*pieces)


def product_kernel(added, tok_ref, spread_ref, *refs):
    early_refs, weight_refs, (out_ref, total_ref) = refs[:added], refs[added:-2], refs[-2:]
    weights = jnp.concatenate([ref[...] for ref in weight_refs], axis=0)
    part = lax.dot_general(
        tok_ref[...], weights, (((1,), (1,)), ((), ())), preferred_element_type=jnp.float32
    )
    step = pl.program_id(0)

    @pl.when(step == 0)
    def _():
        total_ref[...] = part

    @pl.when(step > 0)
    def _():
        total_ref[...] += part

    @pl.when(step == pl.num_programs(0) - 1)
    def _():
        out = jnp.dot(
            total_ref[...].astype(jnp.bfloat16),
            spread_ref[...],
            preferred_element_type=jnp.float32,
        )
        for early_ref in early_refs:
            out = out + early_ref[...].astype(jnp.float32)
        out_ref[...] = out.astype(jnp.bfloat16)


def spread_product(tokens, spread, weights, early=()):
    token_rows, model_width = tokens.shape
    rows, columns = spread.shape
    width = 1024
    whole = lambda n: (0, 0)
    split = lambda n: (0, n)
    body = lambda *refs: product_kernel(len(early), *refs)
    return pl.pallas_call(
        body,
        grid=(model_width // width,),
        in_specs=[
            pl.BlockSpec((token_rows, width), split),
            pl.BlockSpec((rows, columns), whole),
            *[pl.BlockSpec((token_rows, columns), whole) for _ in early],
            *[pl.BlockSpec((value.shape[0], width), split) for value in weights],
        ],
        out_specs=pl.BlockSpec((token_rows, columns), whole),
        out_shape=jax.ShapeDtypeStruct((token_rows, columns), jnp.bfloat16),
        scratch_shapes=[pltpu.VMEM((token_rows, rows), jnp.float32)],
        compiler_params=pltpu.CompilerParams(vmem_limit_bytes=20 << 20),
    )(tokens, spread, *early, *weights)


def interleave_kernel(core_ref, own_ref, peer_ref, out_ref):
    tile = 128
    first = core_ref[0] == 0
    for group in range(own_ref.shape[1] // tile):
        cols = slice(group * tile, (group + 1) * tile)
        own, peer = own_ref[:, cols], peer_ref[:, cols]
        start = 2 * group * tile
        out_ref[:, start : start + tile] = jnp.where(first, own, peer)
        out_ref[:, start + tile : start + 2 * tile] = jnp.where(first, peer, own)


def interleaved(core, own_part, peer_part):
    rows, width = own_part.shape
    whole = pl.BlockSpec(memory_space=pltpu.VMEM)
    return pl.pallas_call(
        interleave_kernel,
        in_specs=[pl.BlockSpec(memory_space=pltpu.SMEM), whole, whole],
        out_specs=whole,
        out_shape=jax.ShapeDtypeStruct((rows, 2 * width), jnp.bfloat16),
        compiler_params=pltpu.CompilerParams(vmem_limit_bytes=8 << 20),
    )(core, own_part, peer_part)


def swapped(value):
    return lax.ppermute(value, "c", [(0, 1), (1, 0)])


def shifted(value, axis_at, shift):
    pairs = []
    for y in range(4):
        for core in range(2):
            for x in range(4):
                along_x = core == axis_at
                to_y, to_x = (y, (x + shift) % 4) if along_x else ((y + shift) % 4, x)
                pairs.append(((y * 2 + core) * 4 + x, (to_y * 2 + core) * 4 + to_x))
    return lax.ppermute(value, FACE, pairs)


def column_spread(place, offsets, count_z, rows_dev):
    core, at_x, at_y = place
    first = jnp.asarray([offset[0] for offset in offsets], jnp.int32)
    second = jnp.asarray([offset[1] for offset in offsets], jnp.int32)
    from_x = (at_x - jnp.where(core == 0, first, second)) % 4
    from_y = (at_y - jnp.where(core == 0, second, first)) % 4
    at_z = jnp.arange(count_z, dtype=jnp.int32)[None, :, None]
    at_j = jnp.arange(rows_dev, dtype=jnp.int32)[None, None, :]
    column = (
        (from_y[:, None, None] * count_z + at_z) * 4 + from_x[:, None, None]
    ) * rows_dev + at_j
    size = 16 * count_z * rows_dev
    return (column.reshape(-1, 1) == jnp.arange(size, dtype=jnp.int32)[None, :]).astype(
        jnp.bfloat16
    )


def shards(
    tokens,
    out_grad,
    master_weights,
    base_weights,
    adam_m,
    adam_v,
    grad_exps,
    diff_exps,
    hadamard_signs,
):
    count_z = lax.axis_size("z")
    rows_dev, model_width = master_weights.shape
    sign_rows = (2 * hadamard_signs - 1).astype(jnp.float32)
    block_len = sign_rows.shape[1]
    matrix = jnp.asarray(hadamard(block_len))
    order = jnp.asarray(row_order(count_z, 4, rows_dev))
    place = [lax.axis_index(axis).reshape(1).astype(jnp.int32) for axis in ("c", "x", "y")]
    exps = grad_exps[0]
    peer_tokens, peer_grad, peer_exps = swapped(tokens), swapped(out_grad), swapped(exps)
    half_matrix, order = matrix.astype(jnp.bfloat16), order.astype(jnp.bfloat16)
    (own,) = coded_gradient(place, tokens, out_grad, hadamard_signs, exps, half_matrix, order)
    halves = []
    for half in (0, 1):
        pair_sums = coded_gradient(
            place,
            peer_tokens,
            peer_grad,
            hadamard_signs,
            peer_exps,
            half_matrix,
            order,
            own=own,
            half=half,
        )
        halves.append([pair_sums[0], *(shifted(pair_sums[far], 0, far) for far in (2, 1, 3))])
    lines = line_sums(*halves)
    face = face_sum([lines[0], *(shifted(lines[far], 1, far) for far in (2, 1, 3))])
    parts = lax.all_to_all(face, "z", 0, 0, tiled=True)
    summed = jnp.sum(parts.astype(jnp.float32), axis=0)
    summed = jnp.swapaxes(summed.reshape(2, rows_dev, -1), 0, 1).reshape(rows_dev, model_width)
    gradient = unrotate_rows(summed, sign_rows, matrix)
    new_master, new_first, new_second = adam_update(gradient, master_weights, adam_m, adam_v)
    owner = lax.axis_index(AXES)
    base_own = lax.dynamic_slice_in_dim(base_weights, owner * rows_dev, rows_dev, 0).astype(
        jnp.float32
    )
    diff_bound = clip_level * jnp.exp2(diff_exps.astype(jnp.float32))
    diff_coded = clip_rows(new_master - base_own, diff_bound).astype(jnp.bfloat16)
    effective = (base_own + diff_coded.astype(jnp.float32)).astype(jnp.bfloat16)
    stacked = lax.all_to_all(
        jnp.broadcast_to(effective[None], (count_z, *effective.shape)), "z", 0, 0, tiled=True
    ).reshape(count_z * rows_dev, model_width)
    order_far = (0, 2, 1, 3)
    face = packed([stacked, *(shifted(stacked, 1, far) for far in order_far[1:])])
    arrived = [shifted(face, 0, far) for far in order_far[1:]]
    spread = column_spread(
        place, [(first, second) for first in order_far for second in order_far], count_z, rows_dev
    )
    near_rows = face.shape[0]
    early = [spread_product(rows, spread[:near_rows], [face]) for rows in (peer_tokens, tokens)]
    early, arrived = lax.optimization_barrier((early, arrived))
    late_spread = spread[near_rows:]
    peer_part = swapped(spread_product(peer_tokens, late_spread, arrived, early[:1]))
    own_part = spread_product(tokens, late_spread, arrived, early[1:])
    projected = interleaved(place[0], own_part, peer_part)
    return (projected, new_master, new_first, new_second)


def solution(mesh):
    split = Mesh(mesh.devices.reshape(4, 2, 8, 4), AXES)
    rows = P(AXES, None)
    return jax.shard_map(
        shards,
        mesh=split,
        in_specs=(rows, rows, rows, P(), rows, rows, P(AXES, None, None), rows, P()),
        out_specs=(rows, rows, rows, rows),
        check_vma=False,
    )
```

```python
import math

import jax
import jax.numpy as jnp
import numpy as np
from jax import lax
from jax.experimental import pallas as pl
from jax.experimental.pallas import tpu as pltpu
from jax.sharding import Mesh
from jax.sharding import PartitionSpec as P

ADAM_STEP = 10
AXES = ("y", "c", "z", "x")
FACE = ("y", "c", "x")

clip_level = 448.0
beta_one = 0.9
beta_two = 0.95
learn_rate = 0.002
decay_rate = 0.1
adam_eps = 1e-08
highest = lax.Precision.HIGHEST


def hadamard(matrix_size):
    positions = np.arange(matrix_size)
    common = positions[:, None] & positions[None, :]
    parity = np.zeros((matrix_size, matrix_size), np.int32)
    for bit_level in range(matrix_size.bit_length() - 1):
        parity = parity + (common >> bit_level & 1)
    return (1 - 2 * (parity % 2)).astype(np.float32)


def unrotate_rows(row_block, sign_rows, matrix):
    row_count = row_block.shape[0]
    turned = jnp.dot(
        row_block.reshape(-1, sign_rows.shape[1]), matrix, precision=highest
    ) / math.sqrt(sign_rows.shape[1])
    return (turned.reshape(row_count, sign_rows.shape[0], sign_rows.shape[1]) * sign_rows).reshape(
        row_block.shape
    )


def clip_rows(row_block, bound_rows):
    row_count = row_block.shape[0]
    shaped = row_block.reshape(row_count, bound_rows.shape[1], -1)
    limits = bound_rows[:, :, None]
    return jnp.clip(shaped, -limits, limits).reshape(row_block.shape)


def adam_update(gradient, master, first, second):
    new_first = beta_one * first + (1.0 - beta_one) * gradient
    new_second = beta_two * second + (1.0 - beta_two) * gradient * gradient
    fix_one = 1.0 - beta_one**ADAM_STEP
    fix_two = 1.0 - beta_two**ADAM_STEP
    step_dir = new_first / fix_one / (jnp.sqrt(new_second / fix_two) + adam_eps)
    new_master = master - learn_rate * (step_dir + decay_rate * master)
    return (new_master, new_first, new_second)


def row_order(count_z, count_x, rows_dev):
    size = count_z * count_x * rows_dev
    spots = np.arange(size)
    at_x, at_z, at_j = spots // (count_z * rows_dev), spots // rows_dev % count_z, spots % rows_dev
    natural = (at_z * count_x + at_x) * rows_dev + at_j
    return (natural[:, None] == spots[None, :]).astype(np.float32)


def coded_kernel(groups, spots, added, offset, core_ref, x_ref, y_ref, tok_ref, *refs):
    grad_refs = refs[:groups]
    sign_ref, exps_ref, mat_ref, order_ref = refs[groups : groups + 4]
    refs = refs[groups + 4 :]
    own_ref = refs[0] if added else None
    out_refs = refs[added:-3]
    turned_ref, grad_t_ref, limit_ref = refs[-3:]
    token_rows, width = tok_ref.shape
    block_len = mat_ref.shape[0]
    tile = order_ref.shape[0]
    part = tile // spots
    core, at_x, at_y = core_ref[0], x_ref[0], y_ref[0]
    first_block = (pl.program_id(0) + offset) * (width // block_len)

    @pl.when(pl.program_id(0) == 0)
    def _():
        for group in range(groups):
            grad_t = lax.dot_general(
                order_ref[...],
                grad_refs[group][...],
                (((1,), (1,)), ((), ())),
                preferred_element_type=jnp.float32,
            ).astype(jnp.bfloat16)
            from_y = lax.rem(group - at_y + groups, groups)
            for spot in range(spots):
                from_x = lax.rem(spot - at_x + spots, spots)
                piece = jnp.where(core == 0, from_x * groups + from_y, from_y * spots + from_x)
                rows = pl.ds(pl.multiple_of(piece * part, part), part)
                values = grad_t[spot * part : (spot + 1) * part]
                grad_t_ref[rows, :token_rows] = values
                grad_t_ref[rows, token_rows:] = values

    levels = (clip_level * jnp.exp2(exps_ref[...].astype(jnp.float32))).astype(jnp.bfloat16)
    spread_shape = (exps_ref.shape[1], width)
    block_at = lax.broadcasted_iota(jnp.int32, spread_shape, 0) - first_block
    lane_at = lax.broadcasted_iota(jnp.int32, spread_shape, 1)
    start_at = block_at * block_len
    inside = (lane_at >= start_at) & (lane_at < start_at + block_len)
    spread = jnp.where(inside, 1.0, 0.0).astype(jnp.bfloat16)
    limit_ref[...] = jnp.dot(levels, spread, preferred_element_type=jnp.float32)

    scale = 1.0 / math.sqrt(block_len)
    for block in range(width // block_len):
        cols = slice(block * block_len, (block + 1) * block_len)
        signs = 2 * sign_ref[pl.ds(first_block + block, 1), :] - 1
        signed = tok_ref[:, cols] * signs.astype(jnp.float32).astype(jnp.bfloat16)
        turned = jnp.dot(signed, mat_ref[...], preferred_element_type=jnp.float32) * scale
        upper = turned.astype(jnp.bfloat16)
        turned_ref[:token_rows, cols] = upper
        turned_ref[token_rows:, cols] = (turned - upper.astype(jnp.float32)).astype(jnp.bfloat16)
    terms = jnp.dot(grad_t_ref[...], turned_ref[...], preferred_element_type=jnp.float32)
    for first in range(4):
        for second in range(4):
            group = lax.rem(at_y + jnp.where(core == 0, second, first), groups)
            start = (first * 4 + second) * part
            rows = slice(start, start + part)
            limit = limit_ref[pl.ds(2 * group + core, 1), :]
            coded = jnp.clip(terms[rows, :], -limit, limit).astype(jnp.bfloat16)
            if not added:
                out_refs[0][rows, :] = coded
                continue
            total = (coded.astype(jnp.float32) + own_ref[rows, :].astype(jnp.float32)).astype(
                jnp.bfloat16
            )
            out_refs[first][second * part : (second + 1) * part, :] = total


def coded_gradient(place, tokens, out_grad, signs, exps, matrix, order, own=None, half=0):
    token_rows, model_width = tokens.shape
    feature_rows = out_grad.shape[1]
    tile = order.shape[0]
    groups = feature_rows // tile // 2
    spots = 4
    width = 1024
    added = own is not None
    heights = [tile] * spots if added else [groups * tile]
    steps = model_width // width // (2 if added else 1)
    offset = half * steps
    whole = lambda n, *place: (0, 0)
    column = lambda n, *place: (0, n + offset)
    placed = lambda n, *place: (0, n)
    grad_spec = lambda group: pl.BlockSpec(
        (token_rows, tile), lambda n, *place: (0, 2 * group + place[0][0])
    )
    in_specs = [
        pl.BlockSpec((token_rows, width), column),
        *[grad_spec(group) for group in range(groups)],
        pl.BlockSpec(signs.shape, whole),
        pl.BlockSpec(exps.shape, whole),
        pl.BlockSpec(matrix.shape, whole),
        pl.BlockSpec(order.shape, whole),
    ]
    operands = [tokens, *[out_grad] * groups, signs, exps, matrix, order]
    if added:
        in_specs.append(pl.BlockSpec((groups * tile, width), column))
        operands.append(own)
    body = lambda *refs: coded_kernel(groups, spots, added, offset, *refs)
    return pl.pallas_call(
        body,
        grid_spec=pltpu.PrefetchScalarGridSpec(
            num_scalar_prefetch=3,
            grid=(steps,),
            in_specs=in_specs,
            out_specs=[pl.BlockSpec((height, width), placed) for height in heights],
            scratch_shapes=[
                pltpu.VMEM((2 * token_rows, width), jnp.bfloat16),
                pltpu.VMEM((groups * tile, 2 * token_rows), jnp.bfloat16),
                pltpu.VMEM((exps.shape[0], width), jnp.float32),
            ],
        ),
        out_shape=[
            jax.ShapeDtypeStruct((height, steps * width), jnp.bfloat16) for height in heights
        ],
        compiler_params=pltpu.CompilerParams(vmem_limit_bytes=(46 if added else 60) << 20),
    )(*place, *operands)


def added_up(refs):
    total = refs[0][...].astype(jnp.float32)
    for ref in refs[1:]:
        total = total + ref[...].astype(jnp.float32)
    return total


def line_kernel(count, *refs):
    out_refs = refs[2 * count :]
    sums = added_up(refs[:count]), added_up(refs[count : 2 * count])
    rows = 8
    pairs = sums[0].shape[0] // rows // len(out_refs)
    for at in range(sums[0].shape[0] // rows):
        left, right = (total[at * rows : (at + 1) * rows] for total in sums)
        upper = lax.broadcasted_iota(jnp.int32, left.shape, 0) < rows // 2
        even = jnp.where(upper, left, pltpu.roll(right, rows // 2, 0))
        odd = jnp.where(upper, pltpu.roll(left, rows // 2, 0), right)
        out_refs[at // pairs][2 * (at % pairs)] = even.astype(jnp.bfloat16)
        out_refs[at // pairs][2 * (at % pairs) + 1] = odd.astype(jnp.bfloat16)


def line_sums(left_terms, right_terms):
    rows, half = left_terms[0].shape
    width = 1024
    count = len(left_terms)
    shape = (rows // 16, 8, half)
    body = lambda *refs: line_kernel(count, *refs)
    return pl.pallas_call(
        body,
        grid=(half // width,),
        in_specs=[pl.BlockSpec((rows, width), lambda n: (0, n))] * (2 * count),
        out_specs=[pl.BlockSpec((*shape[:2], width), lambda n: (0, 0, n))] * 4,
        out_shape=[jax.ShapeDtypeStruct(shape, jnp.bfloat16)] * 4,
        compiler_params=pltpu.CompilerParams(vmem_limit_bytes=16 << 20),
    )(*left_terms, *right_terms)


def face_kernel(*refs):
    refs[-1][...] = added_up(refs[:-1]).astype(jnp.bfloat16)


def face_sum(terms):
    count_z, rows, half = terms[0].shape
    width = 1024
    spec = pl.BlockSpec((count_z, rows, width), lambda n: (0, 0, n))
    return pl.pallas_call(
        face_kernel,
        grid=(half // width,),
        in_specs=[spec] * len(terms),
        out_specs=spec,
        out_shape=jax.ShapeDtypeStruct(terms[0].shape, jnp.bfloat16),
        compiler_params=pltpu.CompilerParams(vmem_limit_bytes=16 << 20),
    )(*terms)


def pack_kernel(*refs):
    rows = refs[0].shape[0]
    for at, ref in enumerate(refs[:-1]):
        refs[-1][at * rows : (at + 1) * rows, :] = ref[...]


def packed(pieces):
    rows, model_width = pieces[0].shape
    whole = pl.BlockSpec(memory_space=pltpu.VMEM)
    return pl.pallas_call(
        pack_kernel,
        in_specs=[whole] * len(pieces),
        out_specs=whole,
        out_shape=jax.ShapeDtypeStruct((len(pieces) * rows, model_width), jnp.bfloat16),
        compiler_params=pltpu.CompilerParams(vmem_limit_bytes=8 << 20),
    )(*pieces)


def product_kernel(offsets, added, core_ref, x_ref, y_ref, tok_ref, *refs):
    early_refs, weight_refs, (out_ref, spread_ref) = refs[:added], refs[added:-2], refs[-2:]
    core, at_x, at_y = core_ref[0], x_ref[0], y_ref[0]
    piece, columns = spread_ref.shape[0] // len(offsets), spread_ref.shape[1]
    row_at = lax.broadcasted_iota(jnp.int32, (piece, columns), 0)
    column_at = lax.broadcasted_iota(jnp.int32, (piece, columns), 1)
    past_start = column_at - ((row_at >> 2) * 16 + (row_at & 3))
    for at, (first, second) in enumerate(offsets):
        from_x = lax.rem(at_x - jnp.where(core == 0, first, second) + 4, 4)
        from_y = lax.rem(at_y - jnp.where(core == 0, second, first) + 4, 4)
        start = from_y * (4 * piece) + from_x * 4
        spread_ref[at * piece : (at + 1) * piece, :] = jnp.where(
            past_start == start, 1.0, 0.0
        ).astype(jnp.bfloat16)
    weights = jnp.concatenate([ref[...] for ref in weight_refs], axis=0)
    total = lax.dot_general(
        tok_ref[...], weights, (((1,), (1,)), ((), ())), preferred_element_type=jnp.float32
    )
    out = jnp.dot(
        total.astype(jnp.bfloat16), spread_ref[...], preferred_element_type=jnp.float32
    )
    for early_ref in early_refs:
        out = out + early_ref[...].astype(jnp.float32)
    out_ref[...] = out.astype(jnp.bfloat16)


def spread_product(place, offsets, tokens, weights, early=()):
    whole = pl.BlockSpec(memory_space=pltpu.VMEM)
    scalar = pl.BlockSpec(memory_space=pltpu.SMEM)
    rows = sum(value.shape[0] for value in weights)
    columns = 16 * (rows // len(offsets))
    body = lambda *refs: product_kernel(offsets, len(early), *refs)
    return pl.pallas_call(
        body,
        in_specs=[scalar] * 3 + [whole] * (1 + len(early) + len(weights)),
        out_specs=whole,
        out_shape=jax.ShapeDtypeStruct((tokens.shape[0], columns), jnp.bfloat16),
        scratch_shapes=[pltpu.VMEM((rows, columns), jnp.bfloat16)],
        compiler_params=pltpu.CompilerParams(vmem_limit_bytes=12 << 20),
    )(*place, tokens, *early, *weights)


def interleave_kernel(core_ref, own_ref, peer_ref, out_ref):
    tile = 128
    first = core_ref[0] == 0
    for group in range(own_ref.shape[1] // tile):
        cols = slice(group * tile, (group + 1) * tile)
        own, peer = own_ref[:, cols], peer_ref[:, cols]
        start = 2 * group * tile
        out_ref[:, start : start + tile] = jnp.where(first, own, peer)
        out_ref[:, start + tile : start + 2 * tile] = jnp.where(first, peer, own)


def interleaved(core, own_part, peer_part):
    rows, width = own_part.shape
    whole = pl.BlockSpec(memory_space=pltpu.VMEM)
    return pl.pallas_call(
        interleave_kernel,
        in_specs=[pl.BlockSpec(memory_space=pltpu.SMEM), whole, whole],
        out_specs=whole,
        out_shape=jax.ShapeDtypeStruct((rows, 2 * width), jnp.bfloat16),
        compiler_params=pltpu.CompilerParams(vmem_limit_bytes=8 << 20),
    )(core, own_part, peer_part)


def swapped(value):
    return lax.ppermute(value, "c", [(0, 1), (1, 0)])


def shifted(value, axis_at, shift):
    pairs = []
    for y in range(4):
        for core in range(2):
            for x in range(4):
                along_x = core == axis_at
                to_y, to_x = (y, (x + shift) % 4) if along_x else ((y + shift) % 4, x)
                pairs.append(((y * 2 + core) * 4 + x, (to_y * 2 + core) * 4 + to_x))
    return lax.ppermute(value, FACE, pairs)


def shards(
    tokens,
    out_grad,
    master_weights,
    base_weights,
    adam_m,
    adam_v,
    grad_exps,
    diff_exps,
    hadamard_signs,
):
    count_z = lax.axis_size("z")
    rows_dev, model_width = master_weights.shape
    sign_rows = (2 * hadamard_signs - 1).astype(jnp.float32)
    block_len = sign_rows.shape[1]
    matrix = jnp.asarray(hadamard(block_len))
    order = jnp.asarray(row_order(count_z, 4, rows_dev))
    place = [lax.axis_index(axis).reshape(1).astype(jnp.int32) for axis in ("c", "x", "y")]
    exps = grad_exps[0]
    peer_tokens, peer_grad, peer_exps = swapped(tokens), swapped(out_grad), swapped(exps)
    half_matrix, order = matrix.astype(jnp.bfloat16), order.astype(jnp.bfloat16)
    (own,) = coded_gradient(place, tokens, out_grad, hadamard_signs, exps, half_matrix, order)
    halves = []
    for half in (0, 1):
        pair_sums = coded_gradient(
            place,
            peer_tokens,
            peer_grad,
            hadamard_signs,
            peer_exps,
            half_matrix,
            order,
            own=own,
            half=half,
        )
        halves.append([pair_sums[0], *(shifted(pair_sums[far], 0, far) for far in (2, 1, 3))])
    lines = line_sums(*halves)
    face = face_sum([lines[0], *(shifted(lines[far], 1, far) for far in (2, 1, 3))])
    parts = lax.all_to_all(face, "z", 0, 0, tiled=True)
    summed = jnp.sum(parts.astype(jnp.float32), axis=0)
    summed = jnp.swapaxes(summed.reshape(2, rows_dev, -1), 0, 1).reshape(rows_dev, model_width)
    gradient = unrotate_rows(summed, sign_rows, matrix)
    new_master, new_first, new_second = adam_update(gradient, master_weights, adam_m, adam_v)
    owner = lax.axis_index(AXES)
    base_own = lax.dynamic_slice_in_dim(base_weights, owner * rows_dev, rows_dev, 0).astype(
        jnp.float32
    )
    diff_bound = clip_level * jnp.exp2(diff_exps.astype(jnp.float32))
    diff_coded = clip_rows(new_master - base_own, diff_bound).astype(jnp.bfloat16)
    effective = (base_own + diff_coded.astype(jnp.float32)).astype(jnp.bfloat16)
    order_far = (0, 2, 1, 3)
    stacked = lax.all_to_all(
        jnp.broadcast_to(effective[None], (count_z, *effective.shape)), "z", 0, 0, tiled=True
    ).reshape(count_z * rows_dev, model_width)
    face = packed([stacked, *(shifted(stacked, 1, far) for far in order_far[1:])])
    arrived = [shifted(face, 0, far) for far in order_far[1:]]
    near = [(0, second) for second in order_far]
    beyond = [(first, second) for first in order_far[1:] for second in order_far]
    early = [spread_product(place, near, rows, [face]) for rows in (peer_tokens, tokens)]
    early, arrived = lax.optimization_barrier((early, arrived))
    peer_part = swapped(spread_product(place, beyond, peer_tokens, arrived, early[:1]))
    own_part = spread_product(place, beyond, tokens, arrived, early[1:])
    projected = interleaved(place[0], own_part, peer_part)
    return (projected, new_master, new_first, new_second)


def solution(mesh):
    split = Mesh(mesh.devices.reshape(4, 2, 8, 4), AXES)
    rows = P(AXES, None)
    return jax.shard_map(
        shards,
        mesh=split,
        in_specs=(rows, rows, rows, P(), rows, rows, P(AXES, None, None), rows, P()),
        out_specs=(rows, rows, rows, rows),
        check_vma=False,
    )
```

```python
import math

import jax
import jax.numpy as jnp
import numpy as np
from jax import lax
from jax.experimental import pallas as pl
from jax.experimental.pallas import tpu as pltpu
from jax.sharding import Mesh
from jax.sharding import PartitionSpec as P

ADAM_STEP = 10
AXES = ("y", "c", "z", "x")
FACE = ("y", "c", "x")

clip_level = 448.0
beta_one = 0.9
beta_two = 0.95
learn_rate = 0.002
decay_rate = 0.1
adam_eps = 1e-08
highest = lax.Precision.HIGHEST


def hadamard(matrix_size):
    positions = np.arange(matrix_size)
    common = positions[:, None] & positions[None, :]
    parity = np.zeros((matrix_size, matrix_size), np.int32)
    for bit_level in range(matrix_size.bit_length() - 1):
        parity = parity + (common >> bit_level & 1)
    return (1 - 2 * (parity % 2)).astype(np.float32)


def unrotate_rows(row_block, sign_rows, matrix):
    row_count = row_block.shape[0]
    turned = jnp.dot(
        row_block.reshape(-1, sign_rows.shape[1]), matrix, precision=highest
    ) / math.sqrt(sign_rows.shape[1])
    return (turned.reshape(row_count, sign_rows.shape[0], sign_rows.shape[1]) * sign_rows).reshape(
        row_block.shape
    )


def clip_rows(row_block, bound_rows):
    row_count = row_block.shape[0]
    shaped = row_block.reshape(row_count, bound_rows.shape[1], -1)
    limits = bound_rows[:, :, None]
    return jnp.clip(shaped, -limits, limits).reshape(row_block.shape)


def adam_update(gradient, master, first, second):
    new_first = beta_one * first + (1.0 - beta_one) * gradient
    new_second = beta_two * second + (1.0 - beta_two) * gradient * gradient
    fix_one = 1.0 - beta_one**ADAM_STEP
    fix_two = 1.0 - beta_two**ADAM_STEP
    step_dir = new_first / fix_one / (jnp.sqrt(new_second / fix_two) + adam_eps)
    new_master = master - learn_rate * (step_dir + decay_rate * master)
    return (new_master, new_first, new_second)


def row_order(count_z, count_x, rows_dev):
    size = count_z * count_x * rows_dev
    spots = np.arange(size)
    at_x, at_z, at_j = spots // (count_z * rows_dev), spots // rows_dev % count_z, spots % rows_dev
    natural = (at_z * count_x + at_x) * rows_dev + at_j
    return (natural[:, None] == spots[None, :]).astype(np.float32)


def coded_kernel(groups, spots, added, offset, core_ref, x_ref, y_ref, tok_ref, *refs):
    grad_refs = refs[:groups]
    sign_ref, exps_ref, mat_ref, order_ref = refs[groups : groups + 4]
    refs = refs[groups + 4 :]
    own_ref = refs[0] if added else None
    out_refs = refs[added:-3]
    turned_ref, grad_t_ref, limit_ref = refs[-3:]
    token_rows, width = tok_ref.shape
    block_len = mat_ref.shape[0]
    tile = order_ref.shape[0]
    part = tile // spots
    core, at_x, at_y = core_ref[0], x_ref[0], y_ref[0]
    first_block = (pl.program_id(0) + offset) * (width // block_len)

    @pl.when(pl.program_id(0) == 0)
    def _():
        for group in range(groups):
            grad_t = lax.dot_general(
                order_ref[...],
                grad_refs[group][...],
                (((1,), (1,)), ((), ())),
                preferred_element_type=jnp.float32,
            ).astype(jnp.bfloat16)
            from_y = lax.rem(group - at_y + groups, groups)
            for spot in range(spots):
                from_x = lax.rem(spot - at_x + spots, spots)
                piece = jnp.where(core == 0, from_x * groups + from_y, from_y * spots + from_x)
                rows = pl.ds(pl.multiple_of(piece * part, part), part)
                values = grad_t[spot * part : (spot + 1) * part]
                grad_t_ref[rows, :token_rows] = values
                grad_t_ref[rows, token_rows:] = values

    levels = (clip_level * jnp.exp2(exps_ref[...].astype(jnp.float32))).astype(jnp.bfloat16)
    spread_shape = (exps_ref.shape[1], width)
    block_at = lax.broadcasted_iota(jnp.int32, spread_shape, 0) - first_block
    lane_at = lax.broadcasted_iota(jnp.int32, spread_shape, 1)
    start_at = block_at * block_len
    inside = (lane_at >= start_at) & (lane_at < start_at + block_len)
    spread = jnp.where(inside, 1.0, 0.0).astype(jnp.bfloat16)
    limit_ref[...] = jnp.dot(levels, spread, preferred_element_type=jnp.float32)

    scale = 1.0 / math.sqrt(block_len)
    for block in range(width // block_len):
        cols = slice(block * block_len, (block + 1) * block_len)
        signs = 2 * sign_ref[pl.ds(first_block + block, 1), :] - 1
        signed = tok_ref[:, cols] * signs.astype(jnp.float32).astype(jnp.bfloat16)
        turned = jnp.dot(signed, mat_ref[...], preferred_element_type=jnp.float32) * scale
        upper = turned.astype(jnp.bfloat16)
        turned_ref[:token_rows, cols] = upper
        turned_ref[token_rows:, cols] = (turned - upper.astype(jnp.float32)).astype(jnp.bfloat16)
    terms = jnp.dot(grad_t_ref[...], turned_ref[...], preferred_element_type=jnp.float32)
    for first in range(4):
        for second in range(4):
            group = lax.rem(at_y + jnp.where(core == 0, second, first), groups)
            start = (first * 4 + second) * part
            rows = slice(start, start + part)
            limit = limit_ref[pl.ds(2 * group + core, 1), :]
            coded = jnp.clip(terms[rows, :], -limit, limit).astype(jnp.bfloat16)
            if not added:
                out_refs[0][rows, :] = coded
                continue
            total = (coded.astype(jnp.float32) + own_ref[rows, :].astype(jnp.float32)).astype(
                jnp.bfloat16
            )
            out_refs[first][second * part : (second + 1) * part, :] = total


def coded_gradient(place, tokens, out_grad, signs, exps, matrix, order, own=None, half=0):
    token_rows, model_width = tokens.shape
    feature_rows = out_grad.shape[1]
    tile = order.shape[0]
    groups = feature_rows // tile // 2
    spots = 4
    width = 1024
    added = own is not None
    heights = [tile] * spots if added else [groups * tile]
    steps = model_width // width // (2 if added else 1)
    offset = half * steps
    whole = lambda n, *place: (0, 0)
    column = lambda n, *place: (0, n + offset)
    placed = lambda n, *place: (0, n)
    grad_spec = lambda group: pl.BlockSpec(
        (token_rows, tile), lambda n, *place: (0, 2 * group + place[0][0])
    )
    in_specs = [
        pl.BlockSpec((token_rows, width), column),
        *[grad_spec(group) for group in range(groups)],
        pl.BlockSpec(signs.shape, whole),
        pl.BlockSpec(exps.shape, whole),
        pl.BlockSpec(matrix.shape, whole),
        pl.BlockSpec(order.shape, whole),
    ]
    operands = [tokens, *[out_grad] * groups, signs, exps, matrix, order]
    if added:
        in_specs.append(pl.BlockSpec((groups * tile, width), column))
        operands.append(own)
    body = lambda *refs: coded_kernel(groups, spots, added, offset, *refs)
    return pl.pallas_call(
        body,
        grid_spec=pltpu.PrefetchScalarGridSpec(
            num_scalar_prefetch=3,
            grid=(steps,),
            in_specs=in_specs,
            out_specs=[pl.BlockSpec((height, width), placed) for height in heights],
            scratch_shapes=[
                pltpu.VMEM((2 * token_rows, width), jnp.bfloat16),
                pltpu.VMEM((groups * tile, 2 * token_rows), jnp.bfloat16),
                pltpu.VMEM((exps.shape[0], width), jnp.float32),
            ],
        ),
        out_shape=[
            jax.ShapeDtypeStruct((height, steps * width), jnp.bfloat16) for height in heights
        ],
        compiler_params=pltpu.CompilerParams(vmem_limit_bytes=(46 if added else 60) << 20),
    )(*place, *operands)


def added_up(refs):
    total = refs[0][...].astype(jnp.float32)
    for ref in refs[1:]:
        total = total + ref[...].astype(jnp.float32)
    return total


def line_kernel(count, *refs):
    out_refs = refs[2 * count :]
    sums = added_up(refs[:count]), added_up(refs[count : 2 * count])
    rows = 8
    pairs = sums[0].shape[0] // rows // len(out_refs)
    for at in range(sums[0].shape[0] // rows):
        left, right = (total[at * rows : (at + 1) * rows] for total in sums)
        upper = lax.broadcasted_iota(jnp.int32, left.shape, 0) < rows // 2
        even = jnp.where(upper, left, pltpu.roll(right, rows // 2, 0))
        odd = jnp.where(upper, pltpu.roll(left, rows // 2, 0), right)
        out_refs[at // pairs][2 * (at % pairs)] = even.astype(jnp.bfloat16)
        out_refs[at // pairs][2 * (at % pairs) + 1] = odd.astype(jnp.bfloat16)


def line_sums(left_terms, right_terms):
    rows, half = left_terms[0].shape
    width = 1024
    count = len(left_terms)
    shape = (rows // 16, 8, half)
    body = lambda *refs: line_kernel(count, *refs)
    return pl.pallas_call(
        body,
        grid=(half // width,),
        in_specs=[pl.BlockSpec((rows, width), lambda n: (0, n))] * (2 * count),
        out_specs=[pl.BlockSpec((*shape[:2], width), lambda n: (0, 0, n))] * 4,
        out_shape=[jax.ShapeDtypeStruct(shape, jnp.bfloat16)] * 4,
        compiler_params=pltpu.CompilerParams(vmem_limit_bytes=16 << 20),
    )(*left_terms, *right_terms)


def face_kernel(*refs):
    refs[-1][...] = added_up(refs[:-1]).astype(jnp.bfloat16)


def face_sum(terms):
    count_z, rows, half = terms[0].shape
    width = 1024
    spec = pl.BlockSpec((count_z, rows, width), lambda n: (0, 0, n))
    return pl.pallas_call(
        face_kernel,
        grid=(half // width,),
        in_specs=[spec] * len(terms),
        out_specs=spec,
        out_shape=jax.ShapeDtypeStruct(terms[0].shape, jnp.bfloat16),
        compiler_params=pltpu.CompilerParams(vmem_limit_bytes=16 << 20),
    )(*terms)


def pack_kernel(*refs):
    *piece_refs, out_ref, flag_ref = refs
    rows = piece_refs[0].shape[0]
    for at, ref in enumerate(piece_refs):
        out_ref[at * rows : (at + 1) * rows, :] = ref[...]
    flag_ref[...] = piece_refs[-1][: flag_ref.shape[0], : flag_ref.shape[1]]


def packed(pieces):
    rows, model_width = pieces[0].shape
    whole = pl.BlockSpec(memory_space=pltpu.VMEM)
    return pl.pallas_call(
        pack_kernel,
        in_specs=[whole] * len(pieces),
        out_specs=[whole, whole],
        out_shape=[
            jax.ShapeDtypeStruct((len(pieces) * rows, model_width), jnp.bfloat16),
            jax.ShapeDtypeStruct((16, 128), jnp.bfloat16),
        ],
        compiler_params=pltpu.CompilerParams(vmem_limit_bytes=8 << 20),
    )(*pieces)


def product_kernel(offsets, added, flags, core_ref, x_ref, y_ref, tok_ref, *refs):
    early_refs, weight_refs = refs[:added], refs[added : -2 - flags]
    out_ref, spread_ref = refs[-2:]
    core, at_x, at_y = core_ref[0], x_ref[0], y_ref[0]
    piece, columns = spread_ref.shape[0] // len(offsets), spread_ref.shape[1]
    row_at = lax.broadcasted_iota(jnp.int32, (piece, columns), 0)
    column_at = lax.broadcasted_iota(jnp.int32, (piece, columns), 1)
    past_start = column_at - ((row_at >> 2) * 16 + (row_at & 3))
    for at, (first, second) in enumerate(offsets):
        from_x = lax.rem(at_x - jnp.where(core == 0, first, second) + 4, 4)
        from_y = lax.rem(at_y - jnp.where(core == 0, second, first) + 4, 4)
        start = from_y * (4 * piece) + from_x * 4
        spread_ref[at * piece : (at + 1) * piece, :] = jnp.where(
            past_start == start, 1.0, 0.0
        ).astype(jnp.bfloat16)
    weights = jnp.concatenate([ref[...] for ref in weight_refs], axis=0)
    total = lax.dot_general(
        tok_ref[...], weights, (((1,), (1,)), ((), ())), preferred_element_type=jnp.float32
    )
    out = jnp.dot(
        total.astype(jnp.bfloat16), spread_ref[...], preferred_element_type=jnp.float32
    )
    for early_ref in early_refs:
        out = out + early_ref[...].astype(jnp.float32)
    out_ref[...] = out.astype(jnp.bfloat16)


def spread_product(place, offsets, tokens, weights, early=(), flag=()):
    whole = pl.BlockSpec(memory_space=pltpu.VMEM)
    scalar = pl.BlockSpec(memory_space=pltpu.SMEM)
    rows = sum(value.shape[0] for value in weights)
    columns = 16 * (rows // len(offsets))
    body = lambda *refs: product_kernel(offsets, len(early), len(flag), *refs)
    return pl.pallas_call(
        body,
        in_specs=[scalar] * 3 + [whole] * (1 + len(early) + len(weights) + len(flag)),
        out_specs=whole,
        out_shape=jax.ShapeDtypeStruct((tokens.shape[0], columns), jnp.bfloat16),
        scratch_shapes=[pltpu.VMEM((rows, columns), jnp.bfloat16)],
        compiler_params=pltpu.CompilerParams(vmem_limit_bytes=12 << 20),
    )(*place, tokens, *early, *weights, *flag)


def interleave_kernel(core_ref, own_ref, peer_ref, out_ref):
    tile = 128
    first = core_ref[0] == 0
    for group in range(own_ref.shape[1] // tile):
        cols = slice(group * tile, (group + 1) * tile)
        own, peer = own_ref[:, cols], peer_ref[:, cols]
        start = 2 * group * tile
        out_ref[:, start : start + tile] = jnp.where(first, own, peer)
        out_ref[:, start + tile : start + 2 * tile] = jnp.where(first, peer, own)


def interleaved(core, own_part, peer_part):
    rows, width = own_part.shape
    whole = pl.BlockSpec(memory_space=pltpu.VMEM)
    return pl.pallas_call(
        interleave_kernel,
        in_specs=[pl.BlockSpec(memory_space=pltpu.SMEM), whole, whole],
        out_specs=whole,
        out_shape=jax.ShapeDtypeStruct((rows, 2 * width), jnp.bfloat16),
        compiler_params=pltpu.CompilerParams(vmem_limit_bytes=8 << 20),
    )(core, own_part, peer_part)


def swapped(value):
    return lax.ppermute(value, "c", [(0, 1), (1, 0)])


def shifted(value, axis_at, shift):
    pairs = []
    for y in range(4):
        for core in range(2):
            for x in range(4):
                along_x = core == axis_at
                to_y, to_x = (y, (x + shift) % 4) if along_x else ((y + shift) % 4, x)
                pairs.append(((y * 2 + core) * 4 + x, (to_y * 2 + core) * 4 + to_x))
    return lax.ppermute(value, FACE, pairs)


def shards(
    tokens,
    out_grad,
    master_weights,
    base_weights,
    adam_m,
    adam_v,
    grad_exps,
    diff_exps,
    hadamard_signs,
):
    count_z = lax.axis_size("z")
    rows_dev, model_width = master_weights.shape
    sign_rows = (2 * hadamard_signs - 1).astype(jnp.float32)
    block_len = sign_rows.shape[1]
    matrix = jnp.asarray(hadamard(block_len))
    order = jnp.asarray(row_order(count_z, 4, rows_dev))
    place = [lax.axis_index(axis).reshape(1).astype(jnp.int32) for axis in ("c", "x", "y")]
    exps = grad_exps[0]
    peer_tokens, peer_grad, peer_exps = swapped(tokens), swapped(out_grad), swapped(exps)
    half_matrix, order = matrix.astype(jnp.bfloat16), order.astype(jnp.bfloat16)
    (own,) = coded_gradient(place, tokens, out_grad, hadamard_signs, exps, half_matrix, order)
    halves = []
    for half in (0, 1):
        pair_sums = coded_gradient(
            place,
            peer_tokens,
            peer_grad,
            hadamard_signs,
            peer_exps,
            half_matrix,
            order,
            own=own,
            half=half,
        )
        halves.append([pair_sums[0], *(shifted(pair_sums[far], 0, far) for far in (2, 1, 3))])
    lines = line_sums(*halves)
    face = face_sum([lines[0], *(shifted(lines[far], 1, far) for far in (2, 1, 3))])
    parts = lax.all_to_all(face, "z", 0, 0, tiled=True)
    summed = jnp.sum(parts.astype(jnp.float32), axis=0)
    summed = jnp.swapaxes(summed.reshape(2, rows_dev, -1), 0, 1).reshape(rows_dev, model_width)
    gradient = unrotate_rows(summed, sign_rows, matrix)
    new_master, new_first, new_second = adam_update(gradient, master_weights, adam_m, adam_v)
    owner = lax.axis_index(AXES)
    base_own = lax.dynamic_slice_in_dim(base_weights, owner * rows_dev, rows_dev, 0).astype(
        jnp.float32
    )
    diff_bound = clip_level * jnp.exp2(diff_exps.astype(jnp.float32))
    diff_coded = clip_rows(new_master - base_own, diff_bound).astype(jnp.bfloat16)
    effective = (base_own + diff_coded.astype(jnp.float32)).astype(jnp.bfloat16)
    order_far = (0, 2, 1, 3)
    stacked = lax.all_to_all(
        jnp.broadcast_to(effective[None], (count_z, *effective.shape)), "z", 0, 0, tiled=True
    ).reshape(count_z * rows_dev, model_width)
    face, flag = packed([stacked, *(shifted(stacked, 1, far) for far in order_far[1:])])
    face, flag = lax.optimization_barrier((face, swapped(flag)))
    arrived = [shifted(face, 0, far) for far in order_far[1:]]
    near = [(0, second) for second in order_far]
    beyond = [(first, second) for first in order_far[1:] for second in order_far]
    early = [
        spread_product(place, near, rows, [face], flag=[flag]) for rows in (peer_tokens, tokens)
    ]
    early, arrived = lax.optimization_barrier((early, arrived))
    peer_part = swapped(spread_product(place, beyond, peer_tokens, arrived, early[:1]))
    own_part = spread_product(place, beyond, tokens, arrived, early[1:])
    projected = interleaved(place[0], own_part, peer_part)
    return (projected, new_master, new_first, new_second)


def solution(mesh):
    split = Mesh(mesh.devices.reshape(4, 2, 8, 4), AXES)
    rows = P(AXES, None)
    return jax.shard_map(
        shards,
        mesh=split,
        in_specs=(rows, rows, rows, P(), rows, rows, P(AXES, None, None), rows, P()),
        out_specs=(rows, rows, rows, rows),
        check_vma=False,
    )
```

```python
import math

import jax
import jax.numpy as jnp
import numpy as np
from jax import lax
from jax.experimental import pallas as pl
from jax.experimental.pallas import tpu as pltpu
from jax.sharding import Mesh
from jax.sharding import PartitionSpec as P

ADAM_STEP = 10
AXES = ("y", "c", "z", "x")
FACE = ("y", "c", "x")

clip_level = 448.0
beta_one = 0.9
beta_two = 0.95
learn_rate = 0.002
decay_rate = 0.1
adam_eps = 1e-08
highest = lax.Precision.HIGHEST


def hadamard(matrix_size):
    positions = np.arange(matrix_size)
    common = positions[:, None] & positions[None, :]
    parity = np.zeros((matrix_size, matrix_size), np.int32)
    for bit_level in range(matrix_size.bit_length() - 1):
        parity = parity + (common >> bit_level & 1)
    return (1 - 2 * (parity % 2)).astype(np.float32)


def update_kernel(parts_ref, sign_ref, mat_ref, master_ref, base_ref, first_ref, second_ref, exps_ref, *refs):
    out_master_ref, out_first_ref, out_second_ref, out_ref, grad_ref, bound_ref = refs
    block_len = mat_ref.shape[0]
    rows, half = master_ref.shape[0], parts_ref.shape[2]
    blocks = half // block_len
    total = parts_ref[0].astype(jnp.float32)
    for at in range(1, parts_ref.shape[0]):
        total = total + parts_ref[at].astype(jnp.float32)
    stacked = jnp.concatenate(
        [total[:, at * block_len : (at + 1) * block_len] for at in range(blocks)], axis=0
    )
    turned = jnp.dot(
        stacked, mat_ref[...], precision=highest, preferred_element_type=jnp.float32
    ) / math.sqrt(block_len)
    signs = (2 * sign_ref[...] - 1).astype(jnp.float32)
    levels = clip_level * jnp.exp2(exps_ref[...].astype(jnp.float32))
    for at in range(blocks):
        piece = turned[2 * rows * at : 2 * rows * (at + 1)]
        for side in range(2):
            block = side * blocks + at
            cols = slice(block * block_len, (block + 1) * block_len)
            grad_ref[:, cols] = piece[side * rows : (side + 1) * rows] * signs[block : block + 1]
            bound_ref[:, cols] = jnp.broadcast_to(levels[:, block : block + 1], (rows, block_len))
    gradient, master = grad_ref[...], master_ref[...]
    new_first = beta_one * first_ref[...] + (1.0 - beta_one) * gradient
    new_second = beta_two * second_ref[...] + (1.0 - beta_two) * gradient * gradient
    fix_one = 1.0 - beta_one**ADAM_STEP
    fix_two = 1.0 - beta_two**ADAM_STEP
    step_dir = new_first / fix_one / (jnp.sqrt(new_second / fix_two) + adam_eps)
    new_master = master - learn_rate * (step_dir + decay_rate * master)
    base, bound = base_ref[...].astype(jnp.float32), bound_ref[...]
    coded = jnp.clip(new_master - base, -bound, bound).astype(jnp.bfloat16)
    effective = (base + coded.astype(jnp.float32)).astype(jnp.bfloat16)
    out_master_ref[...] = new_master
    out_first_ref[...] = new_first
    out_second_ref[...] = new_second
    for at in range(out_ref.shape[0]):
        out_ref[at] = effective


def updated(parts, signs, matrix, master, base, first, second, exps):
    whole = pl.BlockSpec(memory_space=pltpu.VMEM)
    shape = jax.ShapeDtypeStruct(master.shape, jnp.float32)
    copies = jax.ShapeDtypeStruct((parts.shape[0], *master.shape), jnp.bfloat16)
    return pl.pallas_call(
        update_kernel,
        in_specs=[whole] * 8,
        out_specs=[whole] * 4,
        out_shape=[shape, shape, shape, copies],
        scratch_shapes=[pltpu.VMEM(master.shape, jnp.float32)] * 2,
        compiler_params=pltpu.CompilerParams(vmem_limit_bytes=8 << 20),
    )(parts, signs, matrix, master, base, first, second, exps)


def row_order(count_z, count_x, rows_dev):
    size = count_z * count_x * rows_dev
    spots = np.arange(size)
    at_x, at_z, at_j = spots // (count_z * rows_dev), spots // rows_dev % count_z, spots % rows_dev
    natural = (at_z * count_x + at_x) * rows_dev + at_j
    return (natural[:, None] == spots[None, :]).astype(np.float32)


def coded_kernel(groups, spots, added, offset, core_ref, x_ref, y_ref, tok_ref, *refs):
    grad_refs = refs[:groups]
    sign_ref, exps_ref, mat_ref, order_ref = refs[groups : groups + 4]
    refs = refs[groups + 4 :]
    own_ref = refs[0] if added else None
    out_refs = refs[added:-3]
    turned_ref, grad_t_ref, limit_ref = refs[-3:]
    token_rows, width = tok_ref.shape
    block_len = mat_ref.shape[0]
    tile = order_ref.shape[0]
    part = tile // spots
    core, at_x, at_y = core_ref[0], x_ref[0], y_ref[0]
    first_block = (pl.program_id(0) + offset) * (width // block_len)

    @pl.when(pl.program_id(0) == 0)
    def _():
        for group in range(groups):
            grad_t = lax.dot_general(
                order_ref[...],
                grad_refs[group][...],
                (((1,), (1,)), ((), ())),
                preferred_element_type=jnp.float32,
            ).astype(jnp.bfloat16)
            from_y = lax.rem(group - at_y + groups, groups)
            for spot in range(spots):
                from_x = lax.rem(spot - at_x + spots, spots)
                piece = jnp.where(core == 0, from_x * groups + from_y, from_y * spots + from_x)
                rows = pl.ds(pl.multiple_of(piece * part, part), part)
                values = grad_t[spot * part : (spot + 1) * part]
                grad_t_ref[rows, :token_rows] = values
                grad_t_ref[rows, token_rows:] = values

    levels = (clip_level * jnp.exp2(exps_ref[...].astype(jnp.float32))).astype(jnp.bfloat16)
    spread_shape = (exps_ref.shape[1], width)
    block_at = lax.broadcasted_iota(jnp.int32, spread_shape, 0) - first_block
    lane_at = lax.broadcasted_iota(jnp.int32, spread_shape, 1)
    start_at = block_at * block_len
    inside = (lane_at >= start_at) & (lane_at < start_at + block_len)
    spread = jnp.where(inside, 1.0, 0.0).astype(jnp.bfloat16)
    limit_ref[...] = jnp.dot(levels, spread, preferred_element_type=jnp.float32)

    scale = 1.0 / math.sqrt(block_len)
    for block in range(width // block_len):
        cols = slice(block * block_len, (block + 1) * block_len)
        signs = 2 * sign_ref[pl.ds(first_block + block, 1), :] - 1
        signed = tok_ref[:, cols] * signs.astype(jnp.float32).astype(jnp.bfloat16)
        turned = jnp.dot(signed, mat_ref[...], preferred_element_type=jnp.float32) * scale
        upper = turned.astype(jnp.bfloat16)
        turned_ref[:token_rows, cols] = upper
        turned_ref[token_rows:, cols] = (turned - upper.astype(jnp.float32)).astype(jnp.bfloat16)
    terms = jnp.dot(grad_t_ref[...], turned_ref[...], preferred_element_type=jnp.float32)
    for first in range(4):
        for second in range(4):
            group = lax.rem(at_y + jnp.where(core == 0, second, first), groups)
            start = (first * 4 + second) * part
            rows = slice(start, start + part)
            limit = limit_ref[pl.ds(2 * group + core, 1), :]
            coded = jnp.clip(terms[rows, :], -limit, limit).astype(jnp.bfloat16)
            if not added:
                out_refs[0][rows, :] = coded
                continue
            total = (coded.astype(jnp.float32) + own_ref[rows, :].astype(jnp.float32)).astype(
                jnp.bfloat16
            )
            out_refs[first][second * part : (second + 1) * part, :] = total


def coded_gradient(place, tokens, out_grad, signs, exps, matrix, order, own=None, half=0):
    token_rows, model_width = tokens.shape
    feature_rows = out_grad.shape[1]
    tile = order.shape[0]
    groups = feature_rows // tile // 2
    spots = 4
    width = 1024
    added = own is not None
    heights = [tile] * spots if added else [groups * tile]
    steps = model_width // width // (2 if added else 1)
    offset = half * steps
    whole = lambda n, *place: (0, 0)
    column = lambda n, *place: (0, n + offset)
    placed = lambda n, *place: (0, n)
    grad_spec = lambda group: pl.BlockSpec(
        (token_rows, tile), lambda n, *place: (0, 2 * group + place[0][0])
    )
    in_specs = [
        pl.BlockSpec((token_rows, width), column),
        *[grad_spec(group) for group in range(groups)],
        pl.BlockSpec(signs.shape, whole),
        pl.BlockSpec(exps.shape, whole),
        pl.BlockSpec(matrix.shape, whole),
        pl.BlockSpec(order.shape, whole),
    ]
    operands = [tokens, *[out_grad] * groups, signs, exps, matrix, order]
    if added:
        in_specs.append(pl.BlockSpec((groups * tile, width), column))
        operands.append(own)
    body = lambda *refs: coded_kernel(groups, spots, added, offset, *refs)
    return pl.pallas_call(
        body,
        grid_spec=pltpu.PrefetchScalarGridSpec(
            num_scalar_prefetch=3,
            grid=(steps,),
            in_specs=in_specs,
            out_specs=[pl.BlockSpec((height, width), placed) for height in heights],
            scratch_shapes=[
                pltpu.VMEM((2 * token_rows, width), jnp.bfloat16),
                pltpu.VMEM((groups * tile, 2 * token_rows), jnp.bfloat16),
                pltpu.VMEM((exps.shape[0], width), jnp.float32),
            ],
        ),
        out_shape=[
            jax.ShapeDtypeStruct((height, steps * width), jnp.bfloat16) for height in heights
        ],
        compiler_params=pltpu.CompilerParams(vmem_limit_bytes=(46 if added else 60) << 20),
    )(*place, *operands)


def added_up(refs):
    total = refs[0][...].astype(jnp.float32)
    for ref in refs[1:]:
        total = total + ref[...].astype(jnp.float32)
    return total


def line_kernel(count, *refs):
    out_refs = refs[2 * count :]
    sums = added_up(refs[:count]), added_up(refs[count : 2 * count])
    rows = 8
    pairs = sums[0].shape[0] // rows // len(out_refs)
    for at in range(sums[0].shape[0] // rows):
        left, right = (total[at * rows : (at + 1) * rows] for total in sums)
        upper = lax.broadcasted_iota(jnp.int32, left.shape, 0) < rows // 2
        even = jnp.where(upper, left, pltpu.roll(right, rows // 2, 0))
        odd = jnp.where(upper, pltpu.roll(left, rows // 2, 0), right)
        out_refs[at // pairs][2 * (at % pairs)] = even.astype(jnp.bfloat16)
        out_refs[at // pairs][2 * (at % pairs) + 1] = odd.astype(jnp.bfloat16)


def line_sums(left_terms, right_terms):
    rows, half = left_terms[0].shape
    width = 1024
    count = len(left_terms)
    shape = (rows // 16, 8, half)
    body = lambda *refs: line_kernel(count, *refs)
    return pl.pallas_call(
        body,
        grid=(half // width,),
        in_specs=[pl.BlockSpec((rows, width), lambda n: (0, n))] * (2 * count),
        out_specs=[pl.BlockSpec((*shape[:2], width), lambda n: (0, 0, n))] * 4,
        out_shape=[jax.ShapeDtypeStruct(shape, jnp.bfloat16)] * 4,
        compiler_params=pltpu.CompilerParams(vmem_limit_bytes=16 << 20),
    )(*left_terms, *right_terms)


def face_kernel(*refs):
    refs[-1][...] = added_up(refs[:-1]).astype(jnp.bfloat16)


def face_sum(terms):
    count_z, rows, half = terms[0].shape
    width = 1024
    spec = pl.BlockSpec((count_z, rows, width), lambda n: (0, 0, n))
    return pl.pallas_call(
        face_kernel,
        grid=(half // width,),
        in_specs=[spec] * len(terms),
        out_specs=spec,
        out_shape=jax.ShapeDtypeStruct(terms[0].shape, jnp.bfloat16),
        compiler_params=pltpu.CompilerParams(vmem_limit_bytes=16 << 20),
    )(*terms)


def pack_kernel(*refs):
    *piece_refs, out_ref, flag_ref = refs
    rows = piece_refs[0].shape[0]
    for at, ref in enumerate(piece_refs):
        out_ref[at * rows : (at + 1) * rows, :] = ref[...]
    flag_ref[...] = piece_refs[-1][: flag_ref.shape[0], : flag_ref.shape[1]]


def packed(pieces):
    rows, model_width = pieces[0].shape
    whole = pl.BlockSpec(memory_space=pltpu.VMEM)
    return pl.pallas_call(
        pack_kernel,
        in_specs=[whole] * len(pieces),
        out_specs=[whole, whole],
        out_shape=[
            jax.ShapeDtypeStruct((len(pieces) * rows, model_width), jnp.bfloat16),
            jax.ShapeDtypeStruct((16, 128), jnp.bfloat16),
        ],
        compiler_params=pltpu.CompilerParams(vmem_limit_bytes=8 << 20),
    )(*pieces)


def product_kernel(offsets, added, flags, core_ref, x_ref, y_ref, tok_ref, *refs):
    early_refs, weight_refs = refs[:added], refs[added : -2 - flags]
    out_ref, spread_ref = refs[-2:]
    core, at_x, at_y = core_ref[0], x_ref[0], y_ref[0]
    piece, columns = spread_ref.shape[0] // len(offsets), spread_ref.shape[1]
    row_at = lax.broadcasted_iota(jnp.int32, (piece, columns), 0)
    column_at = lax.broadcasted_iota(jnp.int32, (piece, columns), 1)
    past_start = column_at - ((row_at >> 2) * 16 + (row_at & 3))
    for at, (first, second) in enumerate(offsets):
        from_x = lax.rem(at_x - jnp.where(core == 0, first, second) + 4, 4)
        from_y = lax.rem(at_y - jnp.where(core == 0, second, first) + 4, 4)
        start = from_y * (4 * piece) + from_x * 4
        spread_ref[at * piece : (at + 1) * piece, :] = jnp.where(
            past_start == start, 1.0, 0.0
        ).astype(jnp.bfloat16)
    weights = jnp.concatenate([ref[...] for ref in weight_refs], axis=0)
    total = lax.dot_general(
        tok_ref[...], weights, (((1,), (1,)), ((), ())), preferred_element_type=jnp.float32
    )
    out = jnp.dot(
        total.astype(jnp.bfloat16), spread_ref[...], preferred_element_type=jnp.float32
    )
    for early_ref in early_refs:
        out = out + early_ref[...].astype(jnp.float32)
    out_ref[...] = out.astype(jnp.bfloat16)


def spread_product(place, offsets, tokens, weights, early=(), flag=()):
    whole = pl.BlockSpec(memory_space=pltpu.VMEM)
    scalar = pl.BlockSpec(memory_space=pltpu.SMEM)
    rows = sum(value.shape[0] for value in weights)
    columns = 16 * (rows // len(offsets))
    body = lambda *refs: product_kernel(offsets, len(early), len(flag), *refs)
    return pl.pallas_call(
        body,
        in_specs=[scalar] * 3 + [whole] * (1 + len(early) + len(weights) + len(flag)),
        out_specs=whole,
        out_shape=jax.ShapeDtypeStruct((tokens.shape[0], columns), jnp.bfloat16),
        scratch_shapes=[pltpu.VMEM((rows, columns), jnp.bfloat16)],
        compiler_params=pltpu.CompilerParams(vmem_limit_bytes=12 << 20),
    )(*place, tokens, *early, *weights, *flag)


def interleave_kernel(core_ref, own_ref, peer_ref, out_ref):
    tile = 128
    first = core_ref[0] == 0
    for group in range(own_ref.shape[1] // tile):
        cols = slice(group * tile, (group + 1) * tile)
        own, peer = own_ref[:, cols], peer_ref[:, cols]
        start = 2 * group * tile
        out_ref[:, start : start + tile] = jnp.where(first, own, peer)
        out_ref[:, start + tile : start + 2 * tile] = jnp.where(first, peer, own)


def interleaved(core, own_part, peer_part):
    rows, width = own_part.shape
    whole = pl.BlockSpec(memory_space=pltpu.VMEM)
    return pl.pallas_call(
        interleave_kernel,
        in_specs=[pl.BlockSpec(memory_space=pltpu.SMEM), whole, whole],
        out_specs=whole,
        out_shape=jax.ShapeDtypeStruct((rows, 2 * width), jnp.bfloat16),
        compiler_params=pltpu.CompilerParams(vmem_limit_bytes=8 << 20),
    )(core, own_part, peer_part)


def swapped(value):
    return lax.ppermute(value, "c", [(0, 1), (1, 0)])


def shifted(value, axis_at, shift):
    pairs = []
    for y in range(4):
        for core in range(2):
            for x in range(4):
                along_x = core == axis_at
                to_y, to_x = (y, (x + shift) % 4) if along_x else ((y + shift) % 4, x)
                pairs.append(((y * 2 + core) * 4 + x, (to_y * 2 + core) * 4 + to_x))
    return lax.ppermute(value, FACE, pairs)


def shards(
    tokens,
    out_grad,
    master_weights,
    base_weights,
    adam_m,
    adam_v,
    grad_exps,
    diff_exps,
    hadamard_signs,
):
    count_z = lax.axis_size("z")
    rows_dev, model_width = master_weights.shape
    block_len = hadamard_signs.shape[1]
    matrix = jnp.asarray(hadamard(block_len))
    order = jnp.asarray(row_order(count_z, 4, rows_dev))
    place = [lax.axis_index(axis).reshape(1).astype(jnp.int32) for axis in ("c", "x", "y")]
    exps = grad_exps[0]
    peer_tokens, peer_grad, peer_exps = swapped(tokens), swapped(out_grad), swapped(exps)
    half_matrix, order = matrix.astype(jnp.bfloat16), order.astype(jnp.bfloat16)
    (own,) = coded_gradient(place, tokens, out_grad, hadamard_signs, exps, half_matrix, order)
    halves = []
    for half in (0, 1):
        pair_sums = coded_gradient(
            place,
            peer_tokens,
            peer_grad,
            hadamard_signs,
            peer_exps,
            half_matrix,
            order,
            own=own,
            half=half,
        )
        halves.append([pair_sums[0], *(shifted(pair_sums[far], 0, far) for far in (2, 1, 3))])
    lines = line_sums(*halves)
    face = face_sum([lines[0], *(shifted(lines[far], 1, far) for far in (2, 1, 3))])
    parts = lax.all_to_all(face, "z", 0, 0, tiled=True)
    owner = lax.axis_index(AXES)
    base_own = lax.dynamic_slice_in_dim(base_weights, owner * rows_dev, rows_dev, 0)
    new_master, new_first, new_second, effective = updated(
        parts,
        hadamard_signs,
        matrix,
        master_weights,
        base_own,
        adam_m,
        adam_v,
        diff_exps,
    )
    order_far = (0, 2, 1, 3)
    stacked = lax.all_to_all(effective, "z", 0, 0, tiled=True).reshape(-1, model_width)
    face, flag = packed([stacked, *(shifted(stacked, 1, far) for far in order_far[1:])])
    face, flag = lax.optimization_barrier((face, swapped(flag)))
    arrived = [shifted(face, 0, far) for far in order_far[1:]]
    near = [(0, second) for second in order_far]
    beyond = [[(first, second) for second in order_far] for first in order_far[1:]]
    early = [
        spread_product(place, near, rows, [face], flag=[flag]) for rows in (peer_tokens, tokens)
    ]
    early = [
        spread_product(place, beyond[0], rows, arrived[:1], [done])
        for rows, done in zip((peer_tokens, tokens), early)
    ]
    early, last = lax.optimization_barrier((early, arrived[1:]))
    beyond = beyond[1] + beyond[2]
    peer_part = swapped(spread_product(place, beyond, peer_tokens, last, early[:1]))
    own_part = spread_product(place, beyond, tokens, last, early[1:])
    projected = interleaved(place[0], own_part, peer_part)
    return (projected, new_master, new_first, new_second)


def solution(mesh):
    split = Mesh(mesh.devices.reshape(4, 2, 8, 4), AXES)
    rows = P(AXES, None)
    return jax.shard_map(
        shards,
        mesh=split,
        in_specs=(rows, rows, rows, P(), rows, rows, P(AXES, None, None), rows, P()),
        out_specs=(rows, rows, rows, rows),
        check_vma=False,
    )
```
